512 devices in a mesh: fit: 8 (over y, z_hi), ao: 64 (over z_lo, x, core).
Axes of the slice: x: 4, y: 4, z: 16 (z_hi: 2, z_lo: 8; z = z_hi * 8 + z_lo), core: 2. Of those that a mesh axis runs over, the one named last changes fastest.
Arguments:
- occ_blocks: bfloat16 [98304, 512], P(('fit', 'ao')), may hold values from -6 to 6
- resident: bfloat16 [131072, 4096], P(('fit', 'ao')), may hold values from -0.046875 to 0.046875
- row_tiles: int32 [512, 8, 96], P(('fit', 'ao')), may hold values from 0 to 95, as said below
- row_pairs: int32 [3, 512, 8, 96], P(None, ('fit', 'ao')), may hold values from -1 to 31, as said below
- live_rows: int32 [512, 8], P(('fit', 'ao')), may hold values from 1 to 96, as said below
- tile_list: int32 [64, 96], replicated, may hold values from 0 to 1023, as said below
- owner_slot: int32 [256], replicated, may hold values from 0 to 511, as said below
Outputs:
- half_exchange: bfloat16 [512, 64, 512], P('ao', 'fit')
The draws below stay inside these ranges and needn't reach their ends.
Inputs may be any that keep to these rules, and one draw needn't show every extreme that they name: `row_tiles`: within each group and cycle step the 96 entries are a permutation of 0 to 95. `row_pairs`: each entry is a resident tile index, or -1 where the row has no tile for that fitting block; rows at or beyond live_rows are -1. Within a group and cycle step, live rows whose tiles share an AO block name the same resident tile for the same fitting block. `live_rows`: in every draw some group has all 96 rows live at some cycle step. `tile_list`: codes within a column are distinct and name AO blocks that some owner holds. A column names at most 2 tiles whose AO blocks belong to one owner device (owner_slot // 8); in every draw some owner gets exactly 2 from every column. AO blocks take distinct slots; the owner device of block b is owner_slot[b] // 8; an owner holds 0 to 8 blocks in its first slots, and some owner holds exactly 8.
All inputs are finite; a program needn't handle non-finite values.
Results may differ from the reference program's by a relative error of at most 0.001.
Values may be sent and summed in bfloat16 or wider, within the bound.
A program may use at most 64 MiB of HBM per device.

```python
import jax
import jax.numpy as jnp
from jax import lax

OCC = 512
AB = 64
FB = 64
OB = 128
PB_DEV = 3
OWN_CAP = 8
PAIR_STEP = 32
LT = 96
NAOB = 256
NFIT = 98304
N_FIT = 8
N_AO = 64


def ownership(key):
    mean_load = OWN_CAP // 2
    pair_count = N_AO // 2
    imbalance = jax.random.randint(jax.random.fold_in(key, 101), (pair_count,), 0, mean_load)
    imbalance = imbalance.at[0].set(mean_load)
    counts = jnp.stack([mean_load + imbalance, mean_load - imbalance], axis=1).reshape(N_AO).astype(jnp.int32)
    owner_perm = jax.random.permutation(jax.random.fold_in(key, 102), N_AO).astype(jnp.int32)
    owner_perm = ((owner_perm - owner_perm[0] + N_AO - 1) % N_AO).astype(jnp.int32)
    block_perm = jax.random.permutation(jax.random.fold_in(key, 103), NAOB).astype(jnp.int32)
    block_ends = jnp.cumsum(counts).astype(jnp.int32)
    starts = block_ends - counts
    position = jnp.arange(NAOB, dtype=jnp.int32)
    logical = jnp.sum((position[:, None] >= block_ends[None, :]).astype(jnp.int32), axis=1)
    within = position - starts[logical]
    slot_at = owner_perm[logical] * OWN_CAP + within
    owner_table = jnp.zeros((NAOB,), jnp.int32).at[block_perm].set(slot_at)
    return (counts, starts, block_perm, owner_table)


def column_tiles(key):
    counts, starts, block_perm, owner_table = ownership(key)
    occ_count = OCC // OB
    others = N_AO - 2

    def one_column(column):
        column_key = jax.random.fold_in(jax.random.fold_in(key, 201), column)
        order_perm = jax.random.permutation(jax.random.fold_in(column_key, 1), others).astype(jnp.int32) + 2
        flip_bits = jax.random.randint(jax.random.fold_in(column_key, 2), (others // 2,), 0, 2)
        first_share = jnp.where(flip_bits == 1, 2, 1).astype(jnp.int32)
        second_share = 3 - first_share
        first_share = first_share.at[0].set(2)
        second_share = second_share.at[0].set(2)
        wanted = jnp.zeros((N_AO,), jnp.int32).at[order_perm[0::2]].set(first_share)
        wanted = wanted.at[order_perm[1::2]].set(second_share).at[0].set(2)
        option_count = jnp.maximum(counts * occ_count, 1)
        first_pick = jax.random.randint(jax.random.fold_in(column_key, 3), (N_AO,), 0, option_count)
        step_pick = jax.random.randint(jax.random.fold_in(column_key, 4), (N_AO,), 0, jnp.maximum(option_count - 1, 1))
        second_pick = (first_pick + 1 + step_pick) % option_count
        pick_ids = jnp.stack([first_pick, second_pick], axis=1)
        blocks = block_perm[jnp.minimum(starts[:, None] + pick_ids // occ_count, NAOB - 1)]
        tile_codes = blocks * occ_count + pick_ids % occ_count
        is_valid = jnp.arange(2, dtype=jnp.int32)[None, :] < wanted[:, None]
        flat_pos = jnp.arange(2 * N_AO, dtype=jnp.int32).reshape(N_AO, 2)
        sort_score = jnp.where(is_valid, flat_pos, flat_pos + 2 * N_AO).reshape(-1)
        chosen = jnp.argsort(sort_score, stable=True)[:LT]
        row_codes = tile_codes.reshape(-1)[chosen]
        return row_codes[jax.random.permutation(jax.random.fold_in(column_key, 5), LT)].astype(jnp.int32)
    return jax.vmap(one_column)(jnp.arange(N_AO, dtype=jnp.int32))


def live_table(key):
    groups = N_FIT * N_AO
    load_level = jax.random.randint(jax.random.fold_in(key, 301), (groups,), 1, 5)
    heavy_group = jax.random.randint(jax.random.fold_in(key, 302), (), 0, groups)
    load_level = load_level.at[heavy_group].set(4)
    jitter = jax.random.randint(jax.random.fold_in(key, 303), (groups, N_FIT), 0, max(LT // 8, 1))
    counts = jnp.maximum(LT * load_level[:, None] // 4 - jitter, 1)
    full_step = jax.random.randint(jax.random.fold_in(key, 304), (), 0, N_FIT)
    return counts.at[heavy_group, full_step].set(LT).astype(jnp.int32)


def triple_rows(key):
    tiles_all = column_tiles(key)
    live_counts = live_table(key)
    occ_count = OCC // OB
    row_index = jnp.arange(LT, dtype=jnp.int32)

    def one_entry(group_id, cycle_step):
        column = group_id % N_AO
        step_key = jax.random.fold_in(jax.random.fold_in(jax.random.fold_in(key, 401), group_id), cycle_step)
        row_tile = jax.random.permutation(jax.random.fold_in(step_key, 1), LT).astype(jnp.int32)
        blocks = tiles_all[column][row_tile] // occ_count
        is_valid = row_index < live_counts[group_id, cycle_step]
        same_block = (blocks[:, None] == blocks[None, :]) & is_valid[None, :]
        first_row = jnp.min(jnp.where(same_block, row_index[None, :], LT), axis=1)
        present = jax.random.randint(jax.random.fold_in(step_key, 2), (LT, PB_DEV), 0, 3) == 0
        present = present.at[0, 0].set(True)
        present = present & (first_row == row_index)[:, None] & is_valid[:, None]
        present_total = jnp.sum(present.astype(jnp.int32))
        shift_by = jnp.maximum(PAIR_STEP - present_total, 0)
        pair_rank = (jnp.cumsum(present.reshape(-1).astype(jnp.int32)) - 1).reshape(LT, PB_DEV)
        kept_pair = present & (pair_rank < PAIR_STEP)
        slot_pair = jnp.where(kept_pair, pair_rank + shift_by, -1)
        pair_row = slot_pair[jnp.minimum(first_row, LT - 1)]
        pair_row = jnp.where(is_valid[:, None], pair_row, -1)
        return (row_tile, pair_row.T.astype(jnp.int32))
    over_steps = jax.vmap(one_entry, in_axes=(None, 0))
    over_groups = jax.vmap(over_steps, in_axes=(0, None))
    return over_groups(jnp.arange(N_FIT * N_AO, dtype=jnp.int32), jnp.arange(N_FIT, dtype=jnp.int32))


def draw_row_tiles(key, part):
    row_tile, pair_rows = triple_rows(key)
    return row_tile


def draw_row_pairs(key, part):
    row_tile, pair_rows = triple_rows(key)
    return jnp.transpose(pair_rows, (2, 0, 1, 3))


def draw_live_rows(key, part):
    return live_table(key)


def draw_tile_list(key, part):
    tile_rows = column_tiles(key)
    return tile_rows


def draw_owner_slot(key, part):
    return ownership(key)[3]


def block_scale(own_key, shape, shards, smallest, top_value):
    def one(axis_at, shards_of):
        draws = jax.random.uniform(jax.random.fold_in(jax.random.fold_in(own_key, 6), axis_at), (shards_of,), jnp.float32, smallest / len(shards), top_value / len(shards))
        return jnp.repeat(jnp.exp(draws), shape[axis_at] // shards_of).reshape((-1,) + (1,) * (len(shape) - axis_at - 1))

    gain = one(*shards[0])
    for cut in shards[1:]:
        gain = gain * one(*cut)
    return gain


def noise(own_key, dims, deviation, most, shards=(), held_as=jnp.bfloat16):
    gain = block_scale(own_key, dims, shards, -0.22, 0.18) if shards else 1.0
    result = jax.random.normal(own_key, dims, jnp.float32) * deviation * gain
    return jnp.minimum(jnp.maximum(result, -most), most).astype(held_as)


def setup_inputs(seed: int = 0) -> dict:
    seeds = jax.random.split(jax.random.key(seed), 8)
    occ_blocks = noise(seeds[0], (NFIT, OCC), 1.0, 6.0, ((0, 512),))
    resident = noise(seeds[1], (N_FIT * N_AO * N_FIT * PAIR_STEP, AB * FB), (FB * max(1, N_AO * N_FIT * N_FIT * OB // (4 * OCC))) ** -0.5, 0.046875, ((0, 512),))
    row_tiles = draw_row_tiles(jax.random.fold_in(seeds[7], 71), 0)
    row_pairs = draw_row_pairs(jax.random.fold_in(seeds[7], 71), 0)
    live_rows = draw_live_rows(jax.random.fold_in(seeds[7], 71), 0)
    tile_list = draw_tile_list(jax.random.fold_in(seeds[7], 71), 0)
    owner_slot = draw_owner_slot(jax.random.fold_in(seeds[7], 71), 0)
    return dict(occ_blocks=occ_blocks, resident=resident, row_tiles=row_tiles, row_pairs=row_pairs, live_rows=live_rows, tile_list=tile_list, owner_slot=owner_slot)


def reference(occ_blocks, resident, row_tiles, row_pairs, live_rows, tile_list, owner_slot):
    occ_count = OCC // OB
    groups = N_FIT * N_AO
    pieces = occ_blocks.reshape(groups, PB_DEV, FB, occ_count, OB)
    tiles_all = resident.reshape(groups, N_FIT, PAIR_STEP, AB, FB)
    totals = jnp.zeros((N_AO * OWN_CAP, occ_count, AB, OB), jnp.float32)
    row_index = jnp.arange(LT, dtype=jnp.int32)

    def one_group(totals, group_id):
        fit_pos = group_id // N_AO
        column = group_id % N_AO
        tile_codes = tile_list[column]

        def one_step(totals, cycle_step):
            source = ((fit_pos - cycle_step) % N_FIT) * N_AO + column
            upiece = pieces[source]
            tile_ids = row_tiles[group_id, cycle_step]
            pair_ids = row_pairs[:, group_id, cycle_step]
            usable = (pair_ids >= 0) & (row_index < live_rows[group_id, cycle_step])[None, :]
            picked = tiles_all[group_id, cycle_step][jnp.maximum(pair_ids, 0)].astype(jnp.float32)
            picked = jnp.where(usable[:, :, None, None], picked, jnp.zeros((), jnp.float32))
            occ_ids = tile_codes[tile_ids] % occ_count
            chosen = upiece[:, :, occ_ids, :].astype(jnp.float32)
            product = jnp.einsum("jrmp,jprc->rmc", picked, chosen, precision=lax.Precision.HIGHEST)
            slot_ids = owner_slot[tile_codes[tile_ids] // occ_count]
            return totals.at[slot_ids, occ_ids].add(product), None

        totals, _ = lax.scan(one_step, totals, jnp.arange(N_FIT, dtype=jnp.int32))
        return totals, None

    totals, _ = lax.scan(one_group, totals, jnp.arange(groups, dtype=jnp.int32))
    return totals.transpose(0, 2, 1, 3).reshape(N_AO * OWN_CAP, AB, OCC).astype(jnp.bfloat16)
```

```python
import functools

import jax
import jax.numpy as jnp
from jax import lax
from jax.experimental import pallas as pl
from jax.experimental.pallas import tpu as pltpu
from jax.sharding import PartitionSpec as P

AB = 64
FB = 64
OB = 128
OWN_CAP = 8
CAP = 2
NY = 4
NZH = 2
NZL = 8
NXC = 8
UNROLL = 8
MESH = pl.DeviceIdType.MESH
TOP = 32767.0
TINY = 1e-30


def gather_kernel(x_ref, out_ref, send_own, recv_own, send_z, recv_z, send_fw, recv_fw, local_sem):
    fit = lax.axis_index("fit")
    ao = lax.axis_index("ao")
    y, zh = fit // NZH, fit % NZH
    partner = y * NZH + (1 - zh)
    barrier = pltpu.get_barrier_semaphore()
    for d in range(1, NY):
        pl.semaphore_signal(barrier, inc=1, device_id=(((y + d) % NY) * NZH + zh, ao), device_id_type=MESH)
    pl.semaphore_signal(barrier, inc=1, device_id=(partner, ao), device_id_type=MESH)
    pl.semaphore_wait(barrier, NY)

    blocks = x_ref.shape[0] // FB
    across = []
    for j in range(blocks):
        copy = pltpu.make_async_remote_copy(
            src_ref=x_ref.at[pl.ds(j * FB, FB)],
            dst_ref=out_ref.at[fit, pl.ds(j * FB, FB)],
            send_sem=send_z.at[j],
            recv_sem=recv_z.at[j],
            device_id=(partner, ao),
            device_id_type=MESH,
        )
        copy.start()
        across.append(copy)
    own = []
    for d in range(1, NY):
        copy = pltpu.make_async_remote_copy(
            src_ref=x_ref,
            dst_ref=out_ref.at[fit],
            send_sem=send_own.at[d - 1],
            recv_sem=recv_own.at[d - 1],
            device_id=(((y + d) % NY) * NZH + zh, ao),
            device_id_type=MESH,
        )
        copy.start()
        own.append(copy)
    local = pltpu.make_async_copy(x_ref, out_ref.at[fit], local_sem)
    local.start()
    forward = []
    for j in range(blocks):
        across[j].wait_recv()
        for d in range(1, NY):
            copy = pltpu.make_async_remote_copy(
                src_ref=out_ref.at[partner, pl.ds(j * FB, FB)],
                dst_ref=out_ref.at[partner, pl.ds(j * FB, FB)],
                send_sem=send_fw.at[j, d - 1],
                recv_sem=recv_fw.at[j, d - 1],
                device_id=(((y + d) % NY) * NZH + zh, ao),
                device_id_type=MESH,
            )
            copy.start()
            forward.append(copy)
    local.wait()
    for copy in own:
        copy.wait()
    for copy in forward:
        copy.wait()
    for copy in across:
        copy.wait_send()


def gather_occ(occ):
    blocks = occ.shape[0] // FB
    return pl.pallas_call(
        gather_kernel,
        out_shape=jax.ShapeDtypeStruct((NY * NZH,) + occ.shape, occ.dtype),
        in_specs=[pl.BlockSpec(memory_space=pltpu.VMEM)],
        out_specs=pl.BlockSpec(memory_space=pltpu.VMEM),
        scratch_shapes=[
            pltpu.SemaphoreType.DMA((NY - 1,)),
            pltpu.SemaphoreType.DMA((NY - 1,)),
            pltpu.SemaphoreType.DMA((blocks,)),
            pltpu.SemaphoreType.DMA((blocks,)),
            pltpu.SemaphoreType.DMA((blocks, NY - 1)),
            pltpu.SemaphoreType.DMA((blocks, NY - 1)),
            pltpu.SemaphoreType.DMA,
        ],
        compiler_params=pltpu.CompilerParams(collective_id=0, has_side_effects=True, vmem_limit_bytes=16 << 20),
        name="gather_occ",
    )(occ)


def product_kernel(fit_ref, count_ref, list_ref, occ_ref, res_ref, acc_ref, wide):
    fits, rows, occ_width = occ_ref.shape
    blocks, occs = rows // FB, occ_width // OB
    pairs = list_ref.shape[1]
    per_step = res_ref.shape[0] // fits
    wide[...] = jnp.zeros_like(wide)
    acc_ref[...] = jnp.zeros_like(acc_ref)

    def spread(h, _):
        for j in range(blocks):
            for o in range(occs):
                piece = occ_ref[h, j * FB : (j + 1) * FB, o * OB : (o + 1) * OB]
                at = h * (blocks * occs) + j * occs + o
                wide[at, :FB, :OB] = piece
                wide[at, FB:, OB:] = piece
        return 0

    lax.fori_loop(0, fits, spread, 0)
    fit = fit_ref[0]

    def step(s, _):
        base = ((fit - s + fits) % fits) * (blocks * occs)

        def some(i, _):
            done = []
            for u in range(UNROLL):
                code = list_ref[s, i * UNROLL + u]
                a = res_ref[s * per_step + (code & 31)]
                b = wide[base + ((code >> 5) & 15)]
                done.append((code >> 9, jnp.dot(a, b, preferred_element_type=jnp.float32)))
            for t, value in done:
                parts = []
                for y in range(NY):
                    parts.append(value[y * 8 : y * 8 + 8, :OB])
                    parts.append(value[y * 8 : y * 8 + 8, OB:])
                acc_ref[t] += jnp.concatenate(parts, axis=0)
            return 0

        lax.fori_loop(0, (count_ref[s] + UNROLL - 1) // UNROLL, some, 0)
        return 0

    lax.fori_loop(0, fits, step, 0)


def products(fit, counts, codes, occ_all, resident, tiles):
    fits, rows, occ_width = occ_all.shape
    weights = fits * (rows // FB) * (occ_width // OB)
    return pl.pallas_call(
        product_kernel,
        out_shape=jax.ShapeDtypeStruct((tiles + 1, AB, OB), jnp.float32),
        in_specs=[
            pl.BlockSpec(memory_space=pltpu.SMEM),
            pl.BlockSpec(memory_space=pltpu.SMEM),
            pl.BlockSpec(memory_space=pltpu.SMEM),
            pl.BlockSpec(memory_space=pltpu.VMEM),
            pl.BlockSpec(memory_space=pltpu.VMEM),
        ],
        out_specs=pl.BlockSpec(memory_space=pltpu.VMEM),
        scratch_shapes=[pltpu.VMEM((weights, 2 * FB, 2 * OB), jnp.bfloat16)],
        compiler_params=pltpu.CompilerParams(vmem_limit_bytes=32 << 20),
        name="products",
    )(fit, counts, codes, occ_all, resident)


def coded(values):
    top = jnp.maximum(jnp.max(jnp.max(jnp.abs(values), axis=0), axis=0, keepdims=True), TINY)
    whole = jnp.round(values * (TOP / top)[None])
    return whole.astype(jnp.int32).astype(jnp.int16), top * (1.0 / TOP)


def decoded(whole):
    return whole.astype(jnp.int32).astype(jnp.float32)


def reduce_kernel(
    index_ref, acc_ref, target_ref, out_ref,
    qy, sy, ry, rsy, summed, qa, sa, ra, rsa, rb, rsb, flat, final,
    send_y, recv_y, send_a, recv_a, send_b, recv_b,
):
    fit = lax.axis_index("fit")
    ao = lax.axis_index("ao")
    y, zh = fit // NZH, fit % NZH
    zl, xc = ao // NXC, ao % NXC
    z = zh * NZL + zl
    nz = NZH * NZL
    groups = summed.shape[0] // 8

    def at_y(d):
        return (((y + d) % NY) * NZH + zh, ao)

    def at_z(d):
        other = (z + d) % nz
        return other, (y * NZH + other // NZL, (other % NZL) * NXC + xc)

    def at_x(d):
        other = (xc + d) % NXC
        return other, (fit, zl * NXC + other)

    barrier = pltpu.get_barrier_semaphore()
    for d in range(1, NY):
        pl.semaphore_signal(barrier, inc=1, device_id=at_y(d), device_id_type=MESH)
    for d in range(1, nz):
        pl.semaphore_signal(barrier, inc=1, device_id=at_z(d)[1], device_id_type=MESH)
    for d in range(1, NXC):
        pl.semaphore_signal(barrier, inc=1, device_id=at_x(d)[1], device_id_type=MESH)

    copies_y = []
    for d in range(1, NY):
        at = pl.multiple_of(((y + d) % NY) * 16, 16)

        def code_group(g, _, at=at, d=d):
            whole, scale = coded(acc_ref[pl.ds(g * 8, 8), pl.ds(at, 16), :])
            qy[d - 1, pl.ds(g * 8, 8)] = whole
            sy[d - 1, g] = scale
            return 0

        lax.fori_loop(0, groups, code_group, 0)
        if d == 1:
            pl.semaphore_wait(barrier, NY - 1 + nz - 1 + NXC - 1)
        for n, (src, dst) in enumerate(((qy, ry), (sy, rsy))):
            copy = pltpu.make_async_remote_copy(
                src_ref=src.at[d - 1],
                dst_ref=dst.at[d - 1],
                send_sem=send_y.at[n, d - 1],
                recv_sem=recv_y.at[n, d - 1],
                device_id=at_y(d),
                device_id_type=MESH,
            )
            copy.start()
            copies_y.append(copy)
    for copy in copies_y:
        copy.wait_recv()

    mine = pl.multiple_of(y * 16, 16)

    def add_group(g, _):
        total = acc_ref[pl.ds(g * 8, 8), pl.ds(mine, 16), :]
        for d in range(NY - 1):
            total = total + decoded(ry[d, pl.ds(g * 8, 8)]) * rsy[d, g][None]
        summed[pl.ds(g * 8, 8)] = total
        return 0

    lax.fori_loop(0, groups, add_group, 0)

    lower = lax.broadcasted_iota(jnp.int32, (8, OB), 0) < 4

    def pack(block, _):
        firsts, seconds = [], []
        for other in range(NXC):
            halves = ([], [])
            for rank in range(CAP):
                tile = summed[index_ref[(block * NXC + other) * CAP + rank]]
                a, b = tile[:8], tile[8:]
                halves[0].append(jnp.where(lower, a, pltpu.roll(b, 4, 0)))
                halves[1].append(jnp.where(lower, pltpu.roll(a, 4, 0), b))
            firsts.append(jnp.concatenate(halves[0], axis=0)[None])
            seconds.append(jnp.concatenate(halves[1], axis=0)[None])
        for half, values in enumerate((firsts, seconds)):
            whole, scale = coded(jnp.concatenate(values, axis=0))
            qa[half * NZL + block] = whole
            sa[half * NZL + block] = scale
        return 0

    lax.fori_loop(0, NZL, pack, 0)

    copies_a = []
    for d in range(1, nz):
        other, device = at_z(d)
        for n, (src, dst) in enumerate(((qa, ra), (sa, rsa))):
            copy = pltpu.make_async_remote_copy(
                src_ref=src.at[other],
                dst_ref=dst.at[z],
                send_sem=send_a.at[n, d - 1],
                recv_sem=recv_a.at[n, d - 1],
                device_id=device,
                device_id_type=MESH,
            )
            copy.start()
            copies_a.append(copy)
    ra[z] = qa[z]
    rsa[z] = sa[z]
    for copy in copies_a:
        copy.wait_recv()

    copies_b = []
    for d in range(1, NXC):
        other, device = at_x(d)
        for n, (src, dst) in enumerate(((ra.at[:, other], rb.at[xc]), (rsa, rsb.at[xc]))):
            copy = pltpu.make_async_remote_copy(
                src_ref=src,
                dst_ref=dst,
                send_sem=send_b.at[n, d - 1],
                recv_sem=recv_b.at[n, d - 1],
                device_id=device,
                device_id_type=MESH,
            )
            copy.start()
            copies_b.append(copy)
    rb[xc] = ra[:, xc]
    rsb[xc] = rsa[...]
    for copy in copies_b:
        copy.wait_recv()

    def spread(source, _):
        for k in range(nz):
            value = decoded(rb[source, k]) * rsb[source, k]
            flat[pl.ds(pl.multiple_of((source * nz + k) * 16, 16), 16), :] = value
        return 0

    lax.fori_loop(0, NXC, spread, 0)
    entries = NXC * nz * CAP
    occs = out_ref.shape[2] // OB
    names = lax.broadcasted_iota(jnp.int32, (occs * OWN_CAP, entries), 0)
    select = (names == target_ref[...]).astype(jnp.float32)
    for m in range(8):
        part = jnp.dot(
            select, flat[pl.ds(m, entries, stride=8), :],
            precision=lax.Precision.HIGHEST, preferred_element_type=jnp.float32,
        )
        row = 2 * (m % 4) + m // 4
        for o in range(occs):
            final[o, pl.ds(row, OWN_CAP, stride=8), :] = part[o * OWN_CAP : (o + 1) * OWN_CAP]
    for o in range(occs):
        out_ref[:, :, o * OB : (o + 1) * OB] = final[o].reshape(OWN_CAP, 8, OB).astype(out_ref.dtype)
    for copy in copies_y + copies_a + copies_b:
        copy.wait_send()


def reduce_tiles(index, acc, target, occ_width, tiles):
    nz = NZH * NZL
    i16, f32 = jnp.int16, jnp.float32
    return pl.pallas_call(
        reduce_kernel,
        out_shape=jax.ShapeDtypeStruct((OWN_CAP, AB // (NY * NZH), occ_width), jnp.bfloat16),
        in_specs=[
            pl.BlockSpec(memory_space=pltpu.SMEM),
            pl.BlockSpec(memory_space=pltpu.VMEM),
            pl.BlockSpec(memory_space=pltpu.VMEM),
        ],
        out_specs=pl.BlockSpec(memory_space=pltpu.VMEM),
        scratch_shapes=[
            pltpu.VMEM((NY - 1, tiles, 16, OB), i16),
            pltpu.VMEM((NY - 1, tiles // 8, 1, OB), f32),
            pltpu.VMEM((NY - 1, tiles, 16, OB), i16),
            pltpu.VMEM((NY - 1, tiles // 8, 1, OB), f32),
            pltpu.VMEM((tiles, 16, OB), f32),
            pltpu.VMEM((nz, NXC, 16, OB), i16),
            pltpu.VMEM((nz, 1, OB), f32),
            pltpu.VMEM((nz, NXC, 16, OB), i16),
            pltpu.VMEM((nz, 1, OB), f32),
            pltpu.VMEM((NXC, nz, 16, OB), i16),
            pltpu.VMEM((NXC, nz, 1, OB), f32),
            pltpu.VMEM((NXC * nz * 16, OB), f32),
            pltpu.VMEM((occ_width // OB, OWN_CAP * 8, OB), f32),
            pltpu.SemaphoreType.DMA((2, NY - 1)),
            pltpu.SemaphoreType.DMA((2, NY - 1)),
            pltpu.SemaphoreType.DMA((2, nz - 1)),
            pltpu.SemaphoreType.DMA((2, nz - 1)),
            pltpu.SemaphoreType.DMA((2, NXC - 1)),
            pltpu.SemaphoreType.DMA((2, NXC - 1)),
        ],
        compiler_params=pltpu.CompilerParams(collective_id=1, has_side_effects=True, vmem_limit_bytes=32 << 20),
        name="reduce_tiles",
    )(index, acc, target)


def before(n):
    at = jnp.arange(n)
    return (at[:, None] < at[None, :]).astype(jnp.float32)


def pair_list(row_tiles, row_pairs, live_rows, tile_occ):
    blocks, steps, width = row_pairs.shape
    tiles = tile_occ.shape[0]
    usable = (row_pairs >= 0) & (jnp.arange(width) < live_rows[:, None])[None]
    occ_of = jnp.sum(jnp.where(row_tiles[:, :, None] == jnp.arange(tiles), tile_occ, 0), axis=2)
    kinds = jnp.arange(blocks)[:, None, None] * 4 + occ_of[None]
    codes = row_pairs + 32 * kinds + 512 * row_tiles[None]
    usable = usable.transpose(1, 0, 2).reshape(steps, blocks * width)
    codes = codes.transpose(1, 0, 2).reshape(steps, blocks * width)
    place = jnp.dot(usable.astype(jnp.float32), before(blocks * width)).astype(jnp.int32)
    place = jnp.where(usable, place, -1)
    slots = jnp.arange(blocks * width)
    listed = jnp.sum(jnp.where(place[:, None, :] == slots[None, :, None], codes[:, None, :], 0), axis=2)
    counts = jnp.sum(usable.astype(jnp.int32), axis=1)
    return counts, jnp.where(slots[None] < counts[:, None], listed, 512 * tiles)


def routing(tile_list, codes, owner_slot, column, occs):
    blocks = owner_slot.shape[0]
    tiles = codes.shape[0]
    ao_count = tile_list.shape[0]
    numbers = jnp.arange(blocks)
    slots = jnp.sum(jnp.where((codes // occs)[:, None] == numbers, owner_slot, 0), axis=1)
    owners = slots // OWN_CAP
    at = jnp.arange(tiles)
    ranks = jnp.sum(((owners[:, None] == owners[None, :]) & (at[None, :] < at[:, None])).astype(jnp.int32), axis=1)
    places = owners * CAP + ranks
    index = jnp.sum(jnp.where(places[None, :] == jnp.arange(ao_count * CAP)[:, None], at[None, :], 0), axis=1)

    mine = column * OWN_CAP + jnp.arange(OWN_CAP)
    held = jnp.sum(jnp.where(owner_slot[None, :] == mine[:, None], numbers[None, :] + 1, 0), axis=1) - 1
    names = tile_list // occs
    slot = jnp.sum(
        jnp.where(names[:, :, None] == held[None, None, :], jnp.arange(OWN_CAP) + 1, 0), axis=2
    ) - 1
    owned = slot >= 0
    goal = (tile_list % occs) * OWN_CAP + slot
    rank = jnp.dot(owned.astype(jnp.float32), before(tiles)).astype(jnp.int32)
    target = jnp.stack(
        [jnp.sum(jnp.where(owned & (rank == r), goal + 1, 0), axis=1) - 1 for r in range(CAP)], axis=1
    )
    target = target.reshape(NZL, NXC, CAP).transpose(1, 0, 2)
    target = jnp.broadcast_to(target[:, None], (NXC, NZH, NZL, CAP))
    return index, target.reshape(1, -1)


def shards(occ_blocks, resident, row_tiles, row_pairs, live_rows, tile_list, owner_slot):
    column = lax.axis_index("ao")
    fit = lax.axis_index("fit")
    occs = occ_blocks.shape[1] // OB
    codes = lax.dynamic_index_in_dim(tile_list, column, 0, keepdims=False)
    tiles = codes.shape[0]
    counts, listed = pair_list(row_tiles[0], row_pairs[:, 0], live_rows[0], codes % occs)
    index, target = routing(tile_list, codes, owner_slot, column, occs)
    occ_all = gather_occ(occ_blocks)
    rows = resident.reshape(resident.shape[0], AB // 2, 2 * FB)
    acc = products(fit.reshape(1), counts, listed, occ_all, rows, tiles)
    return reduce_tiles(index, acc, target, occ_blocks.shape[1], tiles)


def solution(mesh):
    return jax.shard_map(
        shards,
        mesh=mesh,
        in_specs=(
            P(("fit", "ao"), None),
            P(("fit", "ao"), None),
            P(("fit", "ao"), None, None),
            P(None, ("fit", "ao"), None, None),
            P(("fit", "ao"), None),
            P(),
            P(),
        ),
        out_specs=P("ao", "fit", None),
        check_vma=False,
    )
```

```python
import functools

import jax
import jax.numpy as jnp
from jax import lax
from jax.experimental import pallas as pl
from jax.experimental.pallas import tpu as pltpu
from jax.sharding import PartitionSpec as P

AB = 64
FB = 64
OB = 128
OWN_CAP = 8
CAP = 2
NY = 4
NZH = 2
NZL = 8
NXC = 8
GROUP = 4
MESH = pl.DeviceIdType.MESH
TOP = 32767.0
TINY = 1e-30


def coded(values):
    top = jnp.maximum(jnp.max(jnp.max(jnp.abs(values), axis=0), axis=0, keepdims=True), TINY)
    whole = jnp.round(values * (TOP / top)[None])
    return whole.astype(jnp.int32).astype(jnp.int16), top * (1.0 / TOP)


def decoded(whole):
    return whole.astype(jnp.int32).astype(jnp.float32)


def exchange_kernel(
    table_ref, occ_of_ref, index_ref, x_ref, res_ref, target_ref, out_ref,
    occ_all, wide, res, acc, qy, sy, ry, rsy, qa, sa, ra, rsa, rb, rsb, flat, final,
    send_own, recv_own, send_z, recv_z, send_fw, recv_fw, local_sem,
    send_y, recv_y, send_a, recv_a, send_b, recv_b,
):
    fit = lax.axis_index("fit")
    ao = lax.axis_index("ao")
    y, zh = fit // NZH, fit % NZH
    zl, xc = ao // NXC, ao % NXC
    fits = NY * NZH
    partner = y * NZH + (1 - zh)
    blocks = x_ref.shape[0] // FB
    occs = out_ref.shape[2] // OB
    tiles = res_ref.shape[0]
    per_step = tiles // fits
    half = wide.shape[1] // 2

    def at_y(d):
        return (((y + d) % NY) * NZH + zh, ao)

    def at_z(i, other):
        return (y * NZH + other, ((zl + i) % NZL) * NXC + xc)

    def at_x(d):
        return (fit, zl * NXC + (xc + d) % NXC)

    fill = pltpu.make_async_copy(res_ref, res.at[pl.ds(0, tiles)], local_sem)
    fill.start()
    barrier = pltpu.get_barrier_semaphore()
    pl.semaphore_signal(barrier, inc=1, device_id=(partner, ao), device_id_type=MESH)
    for d in range(1, NY):
        pl.semaphore_signal(barrier, inc=1, device_id=at_y(d), device_id_type=MESH)
    for i in range(1, NZL):
        for other in range(NZH):
            pl.semaphore_signal(barrier, inc=1, device_id=at_z(i, other), device_id_type=MESH)
    for d in range(1, NXC):
        pl.semaphore_signal(barrier, inc=1, device_id=at_x(d), device_id_type=MESH)
    pl.semaphore_wait(barrier, NY + (NZL - 1) * NZH + NXC - 1)

    across = []
    for j in range(blocks):
        copy = pltpu.make_async_remote_copy(
            src_ref=x_ref.at[pl.ds(j * FB, FB)],
            dst_ref=occ_all.at[fit, pl.ds(j * FB, FB)],
            send_sem=send_z.at[j],
            recv_sem=recv_z.at[j],
            device_id=(partner, ao),
            device_id_type=MESH,
        )
        copy.start()
        across.append(copy)
    own = []
    for d in range(1, NY):
        copy = pltpu.make_async_remote_copy(
            src_ref=x_ref,
            dst_ref=occ_all.at[fit],
            send_sem=send_own.at[d - 1],
            recv_sem=recv_own.at[d - 1],
            device_id=at_y(d),
            device_id_type=MESH,
        )
        copy.start()
        own.append(copy)

    wide[...] = jnp.zeros_like(wide)
    res[tiles] = jnp.zeros(res.shape[1:], res.dtype)
    occ_all[fit] = x_ref[...]

    def spread(part):
        def one(i, _):
            source = (fit - (2 * i + part) + fits) % fits
            for j in range(blocks):
                at = pl.multiple_of(part * half + (i * blocks + j) * 2 * FB, 2 * FB)
                for o in range(occs):
                    piece = occ_all[source, j * FB : (j + 1) * FB, o * OB : (o + 1) * OB]
                    wide[o, pl.ds(at, FB), :OB] = piece
                    wide[o, pl.ds(at + FB, FB), OB:] = piece
            return 0

        lax.fori_loop(0, fits // 2, one, 0)

    def multiply(part):
        def one(g, _):
            rows = []
            for u in range(GROUP):
                rows.append(jnp.concatenate(
                    [
                        res[table_ref[j * fits + 2 * i + part, g * GROUP + u]]
                        for i in range(fits // 2)
                        for j in range(blocks)
                    ],
                    axis=1,
                ))
            weights = wide[occ_of_ref[g], part * half : (part + 1) * half, :]
            value = jnp.dot(jnp.concatenate(rows, axis=0), weights, preferred_element_type=jnp.float32)
            height = AB // 2
            for u in range(GROUP):
                parts = []
                for k in range(NY):
                    at = u * height + k * 8
                    parts += [value[at : at + 8, :OB], value[at : at + 8, OB:]]
                tile = jnp.concatenate(parts, axis=0)
                if part == 0:
                    acc[g * GROUP + u] = tile
                else:
                    acc[g * GROUP + u] += tile
            return 0

        lax.fori_loop(0, acc.shape[0] // GROUP, one, 0)

    for copy in own:
        copy.wait_recv()
    spread(0)
    fill.wait()

    forward = []
    multiply(0)
    for j in range(blocks):
        across[j].wait_recv()
        for d in range(1, NY):
            copy = pltpu.make_async_remote_copy(
                src_ref=occ_all.at[partner, pl.ds(j * FB, FB)],
                dst_ref=occ_all.at[partner, pl.ds(j * FB, FB)],
                send_sem=send_fw.at[j, d - 1],
                recv_sem=recv_fw.at[j, d - 1],
                device_id=at_y(d),
                device_id_type=MESH,
            )
            copy.start()
            forward.append(copy)
    for copy in forward:
        copy.wait_recv()
    spread(1)
    multiply(1)

    per_block = NXC * CAP
    groups = per_block // 8

    def copies_y(i):
        made = []
        for d in range(1, NY):
            for n, (src, dst) in enumerate(((qy, ry), (sy, rsy))):
                made.append(pltpu.make_async_remote_copy(
                    src_ref=src.at[i, d - 1],
                    dst_ref=dst.at[i, d - 1],
                    send_sem=send_y.at[i, n, d - 1],
                    recv_sem=recv_y.at[i, n, d - 1],
                    device_id=at_y(d),
                    device_id_type=MESH,
                ))
        return made

    def copies_a(i, other):
        return [
            pltpu.make_async_remote_copy(
                src_ref=src.at[i, other],
                dst_ref=dst.at[i, zh],
                send_sem=send_a.at[i, n, other],
                recv_sem=recv_a.at[i, n, zh],
                device_id=at_z(i, other),
                device_id_type=MESH,
            )
            for n, (src, dst) in enumerate(((qa, ra), (sa, rsa)))
        ]

    def code(i):
        first = ((zl + i) % NZL) * per_block
        for d in range(1, NY):
            at = pl.multiple_of(((y + d) % NY) * 16, 16)
            for g in range(groups):
                values = jnp.concatenate(
                    [acc[index_ref[first + g * 8 + n], pl.ds(at, 16), :][None] for n in range(8)], axis=0
                )
                whole, scale = coded(values)
                qy[i, d - 1, g * 8 : g * 8 + 8] = whole
                sy[i, d - 1, g] = scale
        for copy in copies_y(i):
            copy.start()

    lower = lax.broadcasted_iota(jnp.int32, (8, OB), 0) < 4
    mine = pl.multiple_of(y * 16, 16)

    def collect(i):
        first = ((zl + i) % NZL) * per_block
        for copy in copies_y(i):
            copy.wait_recv()
        firsts, seconds = [], []
        for other in range(NXC):
            halves = ([], [])
            for rank in range(CAP):
                n = other * CAP + rank
                tile = acc[index_ref[first + n], pl.ds(mine, 16), :]
                for d in range(NY - 1):
                    tile = tile + decoded(ry[i, d, n]) * rsy[i, d, n // 8]
                a, b = tile[:8], tile[8:]
                halves[0].append(jnp.where(lower, a, pltpu.roll(b, 4, 0)))
                halves[1].append(jnp.where(lower, pltpu.roll(a, 4, 0), b))
            firsts.append(jnp.concatenate(halves[0], axis=0)[None])
            seconds.append(jnp.concatenate(halves[1], axis=0)[None])
        for k, values in enumerate((firsts, seconds)):
            whole, scale = coded(jnp.concatenate(values, axis=0))
            qa[i, k] = whole
            sa[i, k] = scale

    def send_on(i):
        for other in range(NZH):
            for copy in copies_a(i, other):
                copy.start()

    code(0)
    code(1)
    collect(0)
    first_a = copies_a(0, 1 - zh)
    for copy in first_a:
        copy.start()
    ra[0, zh] = qa[0, zh]
    rsa[0, zh] = sa[0, zh]

    def turn(i, _):
        code(i + 1)
        collect(i)
        send_on(i)
        return 0

    lax.fori_loop(1, NZL - 1, turn, 0)
    collect(NZL - 1)
    send_on(NZL - 1)

    def arrived(i, source):
        for n, dst in enumerate((ra, rsa)):
            pltpu.make_async_remote_copy(
                src_ref=dst.at[i, source],
                dst_ref=dst.at[i, source],
                send_sem=send_a.at[i, n, source],
                recv_sem=recv_a.at[i, n, source],
                device_id=at_z(i, source),
                device_id_type=MESH,
            ).wait_recv()

    def later(i, _):
        for source in range(NZH):
            arrived(i, source)
        return 0

    copies_b = []
    parts = 2
    span = NZL // parts
    for part in range(parts):
        if part == 0:
            arrived(0, 1 - zh)
        lax.fori_loop(max(part * span, 1), (part + 1) * span, later, 0)
        here = pl.ds(part * span, span)
        for d in range(1, NXC):
            other = (xc + d) % NXC
            for n, (src, dst) in enumerate((
                (ra.at[here, :, other], rb.at[xc, here]),
                (rsa.at[here], rsb.at[xc, here]),
            )):
                copy = pltpu.make_async_remote_copy(
                    src_ref=src,
                    dst_ref=dst,
                    send_sem=send_b.at[part, n, d - 1],
                    recv_sem=recv_b.at[part, n, d - 1],
                    device_id=at_x(d),
                    device_id_type=MESH,
                )
                copy.start()
                copies_b.append(copy)
    for i in range(NZL):
        rb[xc, i] = ra[i, :, xc]
    rsb[xc] = rsa[...]
    for copy in copies_b:
        copy.wait_recv()

    def expand(source, _):
        for i in range(NZL):
            for k in range(NZH):
                value = decoded(rb[source, i, k]) * rsb[source, i, k]
                flat[pl.ds(pl.multiple_of(((source * NZL + i) * NZH + k) * 16, 16), 16), :] = value
        return 0

    lax.fori_loop(0, NXC, expand, 0)
    entries = NXC * NZL * NZH * CAP
    names = lax.broadcasted_iota(jnp.int32, (occs * OWN_CAP, entries), 0)
    select = (names == target_ref[...]).astype(jnp.float32)
    for m in range(8):
        part = jnp.dot(
            select, flat[pl.ds(m, entries, stride=8), :],
            precision=lax.Precision.HIGHEST, preferred_element_type=jnp.float32,
        )
        row = 2 * (m % 4) + m // 4
        for o in range(occs):
            final[o, pl.ds(row, OWN_CAP, stride=8), :] = part[o * OWN_CAP : (o + 1) * OWN_CAP]
    for o in range(occs):
        out_ref[:, :, o * OB : (o + 1) * OB] = final[o].reshape(OWN_CAP, 8, OB).astype(out_ref.dtype)

    for copy in across + own + forward + copies_b + first_a:
        copy.wait_send()

    def sent_y(i, _):
        for copy in copies_y(i):
            copy.wait_send()
        return 0

    def sent_a(i, _):
        for other in range(NZH):
            for copy in copies_a(i, other):
                copy.wait_send()
        return 0

    lax.fori_loop(0, NZL, sent_y, 0)
    lax.fori_loop(1, NZL, sent_a, 0)


def exchange(table, occ_of, index, occ, rows, target):
    i16, f32, bf16 = jnp.int16, jnp.float32, jnp.bfloat16
    blocks, occs = occ.shape[0] // FB, occ.shape[1] // OB
    fits = NY * NZH
    slots = table.shape[1]
    dma = pltpu.SemaphoreType.DMA
    smem, vmem = pl.BlockSpec(memory_space=pltpu.SMEM), pl.BlockSpec(memory_space=pltpu.VMEM)
    return pl.pallas_call(
        exchange_kernel,
        out_shape=jax.ShapeDtypeStruct((OWN_CAP, AB // fits, occ.shape[1]), bf16),
        in_specs=[smem, smem, smem, vmem, pl.BlockSpec(memory_space=pl.ANY), vmem],
        out_specs=vmem,
        scratch_shapes=[
            pltpu.VMEM((fits,) + occ.shape, bf16),
            pltpu.VMEM((occs, fits * blocks * 2 * FB, 2 * OB), bf16),
            pltpu.VMEM((rows.shape[0] + 1,) + rows.shape[1:], bf16),
            pltpu.VMEM((slots, AB, OB), f32),
            pltpu.VMEM((NZL, NY - 1, NXC * CAP, 16, OB), i16),
            pltpu.VMEM((NZL, NY - 1, NXC * CAP // 8, 1, OB), f32),
            pltpu.VMEM((NZL, NY - 1, NXC * CAP, 16, OB), i16),
            pltpu.VMEM((NZL, NY - 1, NXC * CAP // 8, 1, OB), f32),
            pltpu.VMEM((NZL, NZH, NXC, 16, OB), i16),
            pltpu.VMEM((NZL, NZH, 1, OB), f32),
            pltpu.VMEM((NZL, NZH, NXC, 16, OB), i16),
            pltpu.VMEM((NZL, NZH, 1, OB), f32),
            pltpu.VMEM((NXC, NZL, NZH, 16, OB), i16),
            pltpu.VMEM((NXC, NZL, NZH, 1, OB), f32),
            pltpu.VMEM((NXC * NZL * NZH * 16, OB), f32),
            pltpu.VMEM((occs, OWN_CAP * 8, OB), f32),
            dma((NY - 1,)), dma((NY - 1,)), dma((blocks,)), dma((blocks,)),
            dma((blocks, NY - 1)), dma((blocks, NY - 1)), dma,
            dma((NZL, 2, NY - 1)), dma((NZL, 2, NY - 1)),
            dma((NZL, 2, NZH)), dma((NZL, 2, NZH)),
            dma((2, 2, NXC - 1)), dma((2, 2, NXC - 1)),
        ],
        compiler_params=pltpu.CompilerParams(collective_id=0, has_side_effects=True, vmem_limit_bytes=48 << 20),
        name="exchange",
    )(table, occ_of, index, occ, rows, target)


def before(n):
    at = jnp.arange(n)
    return (at[:, None] < at[None, :]).astype(jnp.float32)


def earlier_like(values):
    at = jnp.arange(values.shape[0])
    same = (values[:, None] == values[None, :]) & (at[None, :] < at[:, None])
    return jnp.sum(same.astype(jnp.int32), axis=1)


def plan(codes, occs, tiles_slots):
    occ_of = codes % occs
    kinds = jnp.arange(occs)
    counts = jnp.sum((occ_of[None, :] == kinds[:, None]).astype(jnp.int32), axis=1)
    padded = (counts + GROUP - 1) // GROUP * GROUP
    starts = jnp.sum(jnp.where(kinds[None, :] < kinds[:, None], padded[None, :], 0), axis=1)
    slot = earlier_like(occ_of) + jnp.sum(jnp.where(occ_of[:, None] == kinds[None, :], starts[None, :], 0), axis=1)
    firsts = jnp.arange(tiles_slots // GROUP) * GROUP
    group_occ = jnp.sum((firsts[:, None] >= starts[None, :]).astype(jnp.int32), axis=1) - 1
    return slot, group_occ


def pair_table(row_tiles, row_pairs, live_rows, slot, slots, none):
    blocks, steps, width = row_pairs.shape
    per_step = none // steps
    usable = (row_pairs >= 0) & (jnp.arange(width) < live_rows[:, None])[None]
    at = jnp.sum(jnp.where(row_tiles[:, :, None] == jnp.arange(slot.shape[0]), slot, 0), axis=2)
    value = jnp.where(usable, row_pairs + (jnp.arange(steps) * per_step)[None, :, None] - none, 0)
    hit = at[None, :, None, :] == jnp.arange(slots)[None, None, :, None]
    return (jnp.sum(jnp.where(hit, value[:, :, None, :], 0), axis=3) + none).reshape(blocks * steps, slots)


def routing(tile_list, codes, owner_slot, slot, column, occs):
    blocks = owner_slot.shape[0]
    tiles = codes.shape[0]
    ao_count = tile_list.shape[0]
    numbers = jnp.arange(blocks)
    owned_at = jnp.sum(jnp.where((codes // occs)[:, None] == numbers, owner_slot, 0), axis=1)
    owners = owned_at // OWN_CAP
    places = owners * CAP + earlier_like(owners)
    index = jnp.sum(jnp.where(places[None, :] == jnp.arange(ao_count * CAP)[:, None], slot[None, :], 0), axis=1)

    mine = column * OWN_CAP + jnp.arange(OWN_CAP)
    held = jnp.sum(jnp.where(owner_slot[None, :] == mine[:, None], numbers[None, :] + 1, 0), axis=1) - 1
    names = tile_list // occs
    place = jnp.sum(
        jnp.where(names[:, :, None] == held[None, None, :], jnp.arange(OWN_CAP) + 1, 0), axis=2
    ) - 1
    owned = place >= 0
    goal = (tile_list % occs) * OWN_CAP + place
    rank = jnp.dot(owned.astype(jnp.float32), before(tiles)).astype(jnp.int32)
    target = jnp.stack(
        [jnp.sum(jnp.where(owned & (rank == r), goal + 1, 0), axis=1) - 1 for r in range(CAP)], axis=1
    )
    target = target.reshape(NZL, NXC, CAP)
    sources = (column // NXC - jnp.arange(NZL)) % NZL
    turned = jnp.sum(
        jnp.where((sources[:, None] == jnp.arange(NZL)[None, :])[:, :, None, None], target[None], 0), axis=1
    )
    turned = jnp.broadcast_to(turned.transpose(1, 0, 2)[:, :, None], (NXC, NZL, NZH, CAP))
    return index, turned.reshape(1, -1)


def shards(occ_blocks, resident, row_tiles, row_pairs, live_rows, tile_list, owner_slot):
    column = lax.axis_index("ao")
    occs = occ_blocks.shape[1] // OB
    codes = lax.dynamic_index_in_dim(tile_list, column, 0, keepdims=False)
    slots = codes.shape[0] + occs * GROUP
    slot, group_occ = plan(codes, occs, slots)
    table = pair_table(row_tiles[0], row_pairs[:, 0], live_rows[0], slot, slots, resident.shape[0])
    index, target = routing(tile_list, codes, owner_slot, slot, column, occs)
    rows = resident.reshape(resident.shape[0], AB // 2, 2 * FB)
    return exchange(table, group_occ, index, occ_blocks, rows, target)


def solution(mesh):
    return jax.shard_map(
        shards,
        mesh=mesh,
        in_specs=(
            P(("fit", "ao"), None),
            P(("fit", "ao"), None),
            P(("fit", "ao"), None, None),
            P(None, ("fit", "ao"), None, None),
            P(("fit", "ao"), None),
            P(),
            P(),
        ),
        out_specs=P("ao", "fit", None),
        check_vma=False,
    )
```

```python
import functools

import jax
import jax.numpy as jnp
from jax import lax
from jax.experimental import pallas as pl
from jax.experimental.pallas import tpu as pltpu
from jax.sharding import PartitionSpec as P

AB = 64
FB = 64
OB = 128
OWN_CAP = 8
CAP = 2
NY = 4
NZH = 2
NZL = 8
NXC = 8
GROUP = 4
PARTS = 4
MESH = pl.DeviceIdType.MESH
TOP = 32767.0
TINY = 1e-30


def offset(k):
    odd = k % 2
    return odd * ((k + 1) // 2) + (1 - odd) * ((NZL - k // 2) % NZL)


def coded(values):
    top = jnp.maximum(jnp.max(jnp.max(jnp.abs(values), axis=0), axis=0, keepdims=True), TINY)
    whole = jnp.round(values * (TOP / top)[None])
    return whole.astype(jnp.int32).astype(jnp.int16), top * (1.0 / TOP)


def decoded(whole):
    return whole.astype(jnp.int32).astype(jnp.float32)


def exchange_kernel(
    table_ref, occ_of_ref, index_ref, x_ref, res_ref, target_ref, out_ref,
    occ_all, wide, res, acc, qy, sy, ry, rsy, qa, sa, ra, rsa, rb, rsb, flat, summed, final,
    send_own, recv_own, send_z, recv_z, send_fw, recv_fw, local_sem,
    send_y, recv_y, send_a, recv_a, send_b, recv_b,
):
    fit = lax.axis_index("fit")
    ao = lax.axis_index("ao")
    y, zh = fit // NZH, fit % NZH
    zl, xc = ao // NXC, ao % NXC
    fits = NY * NZH
    partner = y * NZH + (1 - zh)
    blocks = x_ref.shape[0] // FB
    occs = out_ref.shape[2] // OB
    tiles = res_ref.shape[0]
    per_step = tiles // fits
    half = wide.shape[1] // 2

    def at_y(d):
        return (((y + d) % NY) * NZH + zh, ao)

    def at_z(i, other):
        return (y * NZH + other, ((zl + offset(i)) % NZL) * NXC + xc)

    def at_x(d):
        return (fit, zl * NXC + (xc + d) % NXC)

    fill = pltpu.make_async_copy(res_ref, res.at[pl.ds(0, tiles)], local_sem)
    fill.start()
    barrier = pltpu.get_barrier_semaphore()
    pl.semaphore_signal(barrier, inc=1, device_id=(partner, ao), device_id_type=MESH)
    for d in range(1, NY):
        pl.semaphore_signal(barrier, inc=1, device_id=at_y(d), device_id_type=MESH)
    for i in range(1, NZL):
        for other in range(NZH):
            pl.semaphore_signal(barrier, inc=1, device_id=at_z(i, other), device_id_type=MESH)
    for d in range(1, NXC):
        pl.semaphore_signal(barrier, inc=1, device_id=at_x(d), device_id_type=MESH)
    pl.semaphore_wait(barrier, NY + (NZL - 1) * NZH + NXC - 1)

    across = []
    for j in range(blocks):
        copy = pltpu.make_async_remote_copy(
            src_ref=x_ref.at[pl.ds(j * FB, FB)],
            dst_ref=occ_all.at[fit, pl.ds(j * FB, FB)],
            send_sem=send_z.at[j],
            recv_sem=recv_z.at[j],
            device_id=(partner, ao),
            device_id_type=MESH,
        )
        copy.start()
        across.append(copy)
    own = []
    for d in range(1, NY):
        copy = pltpu.make_async_remote_copy(
            src_ref=x_ref,
            dst_ref=occ_all.at[fit],
            send_sem=send_own.at[d - 1],
            recv_sem=recv_own.at[d - 1],
            device_id=at_y(d),
            device_id_type=MESH,
        )
        copy.start()
        own.append(copy)

    wide[...] = jnp.zeros_like(wide)
    res[tiles] = jnp.zeros(res.shape[1:], res.dtype)
    occ_all[fit] = x_ref[...]

    def place(part, i, j):
        return (i * blocks + j if part == 0 else (fits // 2) * (blocks + j) + i) * 2 * FB

    def spread(part, wanted):
        def one(i, _):
            source = (fit - (2 * i + part) + fits) % fits
            for j in wanted:
                at = pl.multiple_of(place(part, i, j), 2 * FB)
                for o in range(occs):
                    piece = occ_all[source, j * FB : (j + 1) * FB, o * OB : (o + 1) * OB]
                    wide[o, pl.ds(at, FB), :OB] = piece
                    wide[o, pl.ds(at + FB, FB), OB:] = piece
            return 0

        lax.fori_loop(0, fits // 2, one, 0)

    def multiply(part, wanted, first, last):
        order = [(place(part, i, j), i, j) for i in range(fits // 2) for j in wanted]
        order.sort()
        start = order[0][0]

        def one(g, _):
            rows = []
            for u in range(GROUP):
                rows.append(jnp.concatenate(
                    [res[table_ref[j * fits + 2 * i + part, g * GROUP + u]] for _, i, j in order], axis=1
                ))
            weights = wide[occ_of_ref[g], start : start + len(order) * 2 * FB, :]
            value = jnp.dot(jnp.concatenate(rows, axis=0), weights, preferred_element_type=jnp.float32)
            height = AB // 2
            for u in range(GROUP):
                parts = []
                for k in range(NY):
                    at = u * height + k * 8
                    parts += [value[at : at + 8, :OB], value[at : at + 8, OB:]]
                tile = jnp.concatenate(parts, axis=0)
                if part == 0:
                    acc[g * GROUP + u] = tile
                else:
                    acc[g * GROUP + u] += tile
            return 0

        lax.fori_loop(first, last, one, 0)

    def pass_on(j):
        across[j].wait_recv()
        made = []
        for d in range(1, NY):
            copy = pltpu.make_async_remote_copy(
                src_ref=occ_all.at[partner, pl.ds(j * FB, FB)],
                dst_ref=occ_all.at[partner, pl.ds(j * FB, FB)],
                send_sem=send_fw.at[j, d - 1],
                recv_sem=recv_fw.at[j, d - 1],
                device_id=at_y(d),
                device_id_type=MESH,
            )
            copy.start()
            made.append(copy)
        return made

    for copy in own:
        copy.wait_recv()
    spread(0, range(blocks))
    fill.wait()
    all_groups = acc.shape[0] // GROUP
    multiply(0, range(blocks), 0, all_groups // 2)
    forward = [pass_on(0)]
    multiply(0, range(blocks), all_groups // 2, all_groups)
    for j in range(blocks):
        for copy in forward[j]:
            copy.wait_recv()
        spread(1, [j])
        multiply(1, [j], 0, all_groups)
        if j + 1 < blocks:
            forward.append(pass_on(j + 1))
    forward = [copy for made in forward for copy in made]

    per_block = NXC * CAP
    groups = per_block // 8

    def copies_y(i):
        made = []
        for d in range(1, NY):
            for n, (src, dst) in enumerate(((qy, ry), (sy, rsy))):
                made.append(pltpu.make_async_remote_copy(
                    src_ref=src.at[i, d - 1],
                    dst_ref=dst.at[i, d - 1],
                    send_sem=send_y.at[i, n, d - 1],
                    recv_sem=recv_y.at[i, n, d - 1],
                    device_id=at_y(d),
                    device_id_type=MESH,
                ))
        return made

    def copies_a(i, other):
        return [
            pltpu.make_async_remote_copy(
                src_ref=src.at[i, other],
                dst_ref=dst.at[i, zh],
                send_sem=send_a.at[i, n, other],
                recv_sem=recv_a.at[i, n, zh],
                device_id=at_z(i, other),
                device_id_type=MESH,
            )
            for n, (src, dst) in enumerate(((qa, ra), (sa, rsa)))
        ]

    def code(i):
        first = ((zl + offset(i)) % NZL) * per_block
        for d in range(1, NY):
            at = pl.multiple_of(((y + d) % NY) * 16, 16)
            for g in range(groups):
                values = jnp.concatenate(
                    [acc[index_ref[first + g * 8 + n], pl.ds(at, 16), :][None] for n in range(8)], axis=0
                )
                whole, scale = coded(values)
                qy[i, d - 1, g * 8 : g * 8 + 8] = whole
                sy[i, d - 1, g] = scale
        for copy in copies_y(i):
            copy.start()

    lower = lax.broadcasted_iota(jnp.int32, (8, OB), 0) < 4
    mine = pl.multiple_of(y * 16, 16)

    def collect(i):
        first = ((zl + offset(i)) % NZL) * per_block
        for copy in copies_y(i):
            copy.wait_recv()
        firsts, seconds = [], []
        for other in range(NXC):
            halves = ([], [])
            for rank in range(CAP):
                n = other * CAP + rank
                tile = acc[index_ref[first + n], pl.ds(mine, 16), :]
                for d in range(NY - 1):
                    tile = tile + decoded(ry[i, d, n]) * rsy[i, d, n // 8]
                a, b = tile[:8], tile[8:]
                halves[0].append(jnp.where(lower, a, pltpu.roll(b, 4, 0)))
                halves[1].append(jnp.where(lower, pltpu.roll(a, 4, 0), b))
            firsts.append(jnp.concatenate(halves[0], axis=0)[None])
            seconds.append(jnp.concatenate(halves[1], axis=0)[None])
        for k, values in enumerate((firsts, seconds)):
            whole, scale = coded(jnp.concatenate(values, axis=0))
            qa[i, k] = whole
            sa[i, k] = scale

    def send_on(i):
        for other in range(NZH):
            for copy in copies_a(i, other):
                copy.start()

    code(0)
    code(1)
    collect(0)
    first_a = copies_a(0, 1 - zh)
    for copy in first_a:
        copy.start()
    ra[0, zh] = qa[0, zh]
    rsa[0, zh] = sa[0, zh]

    def turn(i, _):
        code(i + 1)
        collect(i)
        send_on(i)
        return 0

    lax.fori_loop(1, NZL - 1, turn, 0)
    collect(NZL - 1)
    send_on(NZL - 1)

    def arrived(i, source):
        for n, dst in enumerate((ra, rsa)):
            pltpu.make_async_remote_copy(
                src_ref=dst.at[i, source],
                dst_ref=dst.at[i, source],
                send_sem=send_a.at[i, n, source],
                recv_sem=recv_a.at[i, n, source],
                device_id=at_z(i, source),
                device_id_type=MESH,
            ).wait_recv()

    def later(i, _):
        for source in range(NZH):
            arrived(i, source)
        return 0

    span = NZL // PARTS
    entries = NXC * span * NZH * CAP
    names = lax.broadcasted_iota(jnp.int32, (occs * OWN_CAP, entries), 0)
    copies_b = []

    def send_x(part):
        if part == 0:
            arrived(0, 1 - zh)
        lax.fori_loop(max(part * span, 1), (part + 1) * span, later, 0)
        here = pl.ds(part * span, span)
        made = []
        for d in range(1, NXC):
            other = (xc + d) % NXC
            for n, (src, dst) in enumerate((
                (ra.at[here, :, other], rb.at[part, xc]),
                (rsa.at[here], rsb.at[part, xc]),
            )):
                copy = pltpu.make_async_remote_copy(
                    src_ref=src,
                    dst_ref=dst,
                    send_sem=send_b.at[part, n, d - 1],
                    recv_sem=recv_b.at[part, n, d - 1],
                    device_id=at_x(d),
                    device_id_type=MESH,
                )
                copy.start()
                made.append(copy)
        for i in range(span):
            rb[part, xc, i] = ra[part * span + i, :, xc]
            rsb[part, xc, i] = rsa[part * span + i]
        copies_b.append(made)

    def add_up(part):
        for copy in copies_b[part]:
            copy.wait_recv()

        def expand(source, _):
            for i in range(span):
                for k in range(NZH):
                    value = decoded(rb[part, source, i, k]) * rsb[part, source, i, k]
                    flat[part, pl.ds(pl.multiple_of(((source * span + i) * NZH + k) * 16, 16), 16), :] = value
            return 0

        lax.fori_loop(0, NXC, expand, 0)
        select = (names == target_ref[part : part + 1, :]).astype(jnp.float32)
        for m in range(8):
            total = jnp.dot(
                select, flat[part, pl.ds(m, entries, stride=8), :],
                precision=lax.Precision.HIGHEST, preferred_element_type=jnp.float32,
            )
            if part:
                total += summed[m]
            if part + 1 < PARTS:
                summed[m] = total
                continue
            row = 2 * (m % 4) + m // 4
            for o in range(occs):
                final[o, pl.ds(row, OWN_CAP, stride=8), :] = total[o * OWN_CAP : (o + 1) * OWN_CAP]

    for part in range(PARTS):
        send_x(part)
        if part:
            add_up(part - 1)
    add_up(PARTS - 1)
    copies_b = [copy for made in copies_b for copy in made]
    for o in range(occs):
        out_ref[:, :, o * OB : (o + 1) * OB] = final[o].reshape(OWN_CAP, 8, OB).astype(out_ref.dtype)

    for copy in across + own + forward + copies_b + first_a:
        copy.wait_send()

    def sent_y(i, _):
        for copy in copies_y(i):
            copy.wait_send()
        return 0

    def sent_a(i, _):
        for other in range(NZH):
            for copy in copies_a(i, other):
                copy.wait_send()
        return 0

    lax.fori_loop(0, NZL, sent_y, 0)
    lax.fori_loop(1, NZL, sent_a, 0)


def exchange(table, occ_of, index, occ, rows, target):
    i16, f32, bf16 = jnp.int16, jnp.float32, jnp.bfloat16
    blocks, occs = occ.shape[0] // FB, occ.shape[1] // OB
    fits = NY * NZH
    slots = table.shape[1]
    dma = pltpu.SemaphoreType.DMA
    smem, vmem = pl.BlockSpec(memory_space=pltpu.SMEM), pl.BlockSpec(memory_space=pltpu.VMEM)
    return pl.pallas_call(
        exchange_kernel,
        out_shape=jax.ShapeDtypeStruct((OWN_CAP, AB // fits, occ.shape[1]), bf16),
        in_specs=[smem, smem, smem, vmem, pl.BlockSpec(memory_space=pl.ANY), vmem],
        out_specs=vmem,
        scratch_shapes=[
            pltpu.VMEM((fits,) + occ.shape, bf16),
            pltpu.VMEM((occs, fits * blocks * 2 * FB, 2 * OB), bf16),
            pltpu.VMEM((rows.shape[0] + 1,) + rows.shape[1:], bf16),
            pltpu.VMEM((slots, AB, OB), f32),
            pltpu.VMEM((NZL, NY - 1, NXC * CAP, 16, OB), i16),
            pltpu.VMEM((NZL, NY - 1, NXC * CAP // 8, 1, OB), f32),
            pltpu.VMEM((NZL, NY - 1, NXC * CAP, 16, OB), i16),
            pltpu.VMEM((NZL, NY - 1, NXC * CAP // 8, 1, OB), f32),
            pltpu.VMEM((NZL, NZH, NXC, 16, OB), i16),
            pltpu.VMEM((NZL, NZH, 1, OB), f32),
            pltpu.VMEM((NZL, NZH, NXC, 16, OB), i16),
            pltpu.VMEM((NZL, NZH, 1, OB), f32),
            pltpu.VMEM((PARTS, NXC, NZL // PARTS, NZH, 16, OB), i16),
            pltpu.VMEM((PARTS, NXC, NZL // PARTS, NZH, 1, OB), f32),
            pltpu.VMEM((PARTS, NXC * NZL // PARTS * NZH * 16, OB), f32),
            pltpu.VMEM((8, occs * OWN_CAP, OB), f32),
            pltpu.VMEM((occs, OWN_CAP * 8, OB), f32),
            dma((NY - 1,)), dma((NY - 1,)), dma((blocks,)), dma((blocks,)),
            dma((blocks, NY - 1)), dma((blocks, NY - 1)), dma,
            dma((NZL, 2, NY - 1)), dma((NZL, 2, NY - 1)),
            dma((NZL, 2, NZH)), dma((NZL, 2, NZH)),
            dma((PARTS, 2, NXC - 1)), dma((PARTS, 2, NXC - 1)),
        ],
        compiler_params=pltpu.CompilerParams(collective_id=0, has_side_effects=True, vmem_limit_bytes=48 << 20),
        name="exchange",
    )(table, occ_of, index, occ, rows, target)


def before(n):
    at = jnp.arange(n)
    return (at[:, None] < at[None, :]).astype(jnp.float32)


def earlier_like(values):
    at = jnp.arange(values.shape[0])
    same = (values[:, None] == values[None, :]) & (at[None, :] < at[:, None])
    return jnp.sum(same.astype(jnp.int32), axis=1)


def plan(codes, occs, tiles_slots):
    occ_of = codes % occs
    kinds = jnp.arange(occs)
    counts = jnp.sum((occ_of[None, :] == kinds[:, None]).astype(jnp.int32), axis=1)
    padded = (counts + GROUP - 1) // GROUP * GROUP
    starts = jnp.sum(jnp.where(kinds[None, :] < kinds[:, None], padded[None, :], 0), axis=1)
    slot = earlier_like(occ_of) + jnp.sum(jnp.where(occ_of[:, None] == kinds[None, :], starts[None, :], 0), axis=1)
    firsts = jnp.arange(tiles_slots // GROUP) * GROUP
    group_occ = jnp.sum((firsts[:, None] >= starts[None, :]).astype(jnp.int32), axis=1) - 1
    return slot, group_occ


def pair_table(row_tiles, row_pairs, live_rows, slot, slots, none):
    blocks, steps, width = row_pairs.shape
    per_step = none // steps
    usable = (row_pairs >= 0) & (jnp.arange(width) < live_rows[:, None])[None]
    at = jnp.sum(jnp.where(row_tiles[:, :, None] == jnp.arange(slot.shape[0]), slot, 0), axis=2)
    value = jnp.where(usable, row_pairs + (jnp.arange(steps) * per_step)[None, :, None] - none, 0)
    hit = at[None, :, None, :] == jnp.arange(slots)[None, None, :, None]
    return (jnp.sum(jnp.where(hit, value[:, :, None, :], 0), axis=3) + none).reshape(blocks * steps, slots)


def routing(tile_list, codes, owner_slot, slot, column, occs):
    blocks = owner_slot.shape[0]
    tiles = codes.shape[0]
    ao_count = tile_list.shape[0]
    numbers = jnp.arange(blocks)
    owned_at = jnp.sum(jnp.where((codes // occs)[:, None] == numbers, owner_slot, 0), axis=1)
    owners = owned_at // OWN_CAP
    places = owners * CAP + earlier_like(owners)
    index = jnp.sum(jnp.where(places[None, :] == jnp.arange(ao_count * CAP)[:, None], slot[None, :], 0), axis=1)

    mine = column * OWN_CAP + jnp.arange(OWN_CAP)
    held = jnp.sum(jnp.where(owner_slot[None, :] == mine[:, None], numbers[None, :] + 1, 0), axis=1) - 1
    names = tile_list // occs
    place = jnp.sum(
        jnp.where(names[:, :, None] == held[None, None, :], jnp.arange(OWN_CAP) + 1, 0), axis=2
    ) - 1
    owned = place >= 0
    goal = (tile_list % occs) * OWN_CAP + place
    rank = jnp.dot(owned.astype(jnp.float32), before(tiles)).astype(jnp.int32)
    target = jnp.stack(
        [jnp.sum(jnp.where(owned & (rank == r), goal + 1, 0), axis=1) - 1 for r in range(CAP)], axis=1
    )
    target = target.reshape(NZL, NXC, CAP)
    sources = (column // NXC - offset(jnp.arange(NZL))) % NZL
    turned = jnp.sum(
        jnp.where((sources[:, None] == jnp.arange(NZL)[None, :])[:, :, None, None], target[None], 0), axis=1
    )
    turned = turned.reshape(PARTS, NZL // PARTS, NXC, CAP).transpose(0, 2, 1, 3)
    turned = jnp.broadcast_to(turned[:, :, :, None], (PARTS, NXC, NZL // PARTS, NZH, CAP))
    return index, turned.reshape(PARTS, -1)


def shards(occ_blocks, resident, row_tiles, row_pairs, live_rows, tile_list, owner_slot):
    column = lax.axis_index("ao")
    occs = occ_blocks.shape[1] // OB
    codes = lax.dynamic_index_in_dim(tile_list, column, 0, keepdims=False)
    slots = codes.shape[0] + occs * GROUP
    slot, group_occ = plan(codes, occs, slots)
    table = pair_table(row_tiles[0], row_pairs[:, 0], live_rows[0], slot, slots, resident.shape[0])
    index, target = routing(tile_list, codes, owner_slot, slot, column, occs)
    rows = resident.reshape(resident.shape[0], AB // 2, 2 * FB)
    return exchange(table, group_occ, index, occ_blocks, rows, target)


def solution(mesh):
    return jax.shard_map(
        shards,
        mesh=mesh,
        in_specs=(
            P(("fit", "ao"), None),
            P(("fit", "ao"), None),
            P(("fit", "ao"), None, None),
            P(None, ("fit", "ao"), None, None),
            P(("fit", "ao"), None),
            P(),
            P(),
        ),
        out_specs=P("ao", "fit", None),
        check_vma=False,
    )
```

```python
import functools

import jax
import jax.numpy as jnp
from jax import lax
from jax.experimental import pallas as pl
from jax.experimental.pallas import tpu as pltpu
from jax.sharding import PartitionSpec as P

AB = 64
FB = 64
OB = 128
OWN_CAP = 8
CAP = 2
NY = 4
NZH = 2
NZL = 8
NXC = 8
GROUP = 4
PARTS = 4
TOGETHER = 4
TILES = 96
OCCS = 4
OCC_BITS = 2
PAIRS = 32
MESH = pl.DeviceIdType.MESH
TOP = 32767.0
TINY = 1e-30


def offset(k):
    odd = k % 2
    return odd * ((k + 1) // 2) + (1 - odd) * ((NZL - k // 2) % NZL)


def coded(values):
    top = jnp.maximum(jnp.max(jnp.max(jnp.abs(values), axis=0), axis=0, keepdims=True), TINY)
    whole = jnp.round(values * (TOP / top)[None])
    return whole.astype(jnp.int32).astype(jnp.int16), top * (1.0 / TOP)


def decoded(whole):
    return whole.astype(jnp.int32).astype(jnp.float32)


def exchange_kernel(
    plan_ref, x_ref, res_ref, target_ref, out_ref,
    occ_all, wide, res, acc, qy, sy, ry, rsy, qa, sa, ra, rsa, rb, rsb, flat, summed, final,
    send_own, recv_own, send_z, recv_z, send_fw, recv_fw, local_sem,
    send_y, recv_y, send_a, recv_a, send_b, recv_b,
):
    fit = lax.axis_index("fit")
    ao = lax.axis_index("ao")
    y, zh = fit // NZH, fit % NZH
    zl, xc = ao // NXC, ao % NXC
    fits = NY * NZH
    partner = y * NZH + (1 - zh)
    blocks = x_ref.shape[0] // FB
    occs = out_ref.shape[2] // OB
    tiles = res_ref.shape[0]
    per_step = tiles // fits
    half = wide.shape[1] // 2

    def at_y(d):
        return (((y + d) % NY) * NZH + zh, ao)

    def at_z(i, other):
        return (y * NZH + other, ((zl + offset(i)) % NZL) * NXC + xc)

    def at_x(d):
        return (fit, zl * NXC + (xc + d) % NXC)

    fill = pltpu.make_async_copy(res_ref, res.at[pl.ds(0, tiles)], local_sem)
    fill.start()
    barrier = pltpu.get_barrier_semaphore()
    pl.semaphore_signal(barrier, inc=1, device_id=(partner, ao), device_id_type=MESH)
    for d in range(1, NY):
        pl.semaphore_signal(barrier, inc=1, device_id=at_y(d), device_id_type=MESH)
    for i in range(1, NZL):
        for other in range(NZH):
            pl.semaphore_signal(barrier, inc=1, device_id=at_z(i, other), device_id_type=MESH)
    for d in range(1, NXC):
        pl.semaphore_signal(barrier, inc=1, device_id=at_x(d), device_id_type=MESH)
    pl.semaphore_wait(barrier, NY + (NZL - 1) * NZH + NXC - 1)

    across = []
    for j in range(blocks):
        copy = pltpu.make_async_remote_copy(
            src_ref=x_ref.at[pl.ds(j * FB, FB)],
            dst_ref=occ_all.at[fit, pl.ds(j * FB, FB)],
            send_sem=send_z.at[j],
            recv_sem=recv_z.at[j],
            device_id=(partner, ao),
            device_id_type=MESH,
        )
        copy.start()
        across.append(copy)
    own = []
    for d in range(1, NY):
        copy = pltpu.make_async_remote_copy(
            src_ref=x_ref,
            dst_ref=occ_all.at[fit],
            send_sem=send_own.at[d - 1],
            recv_sem=recv_own.at[d - 1],
            device_id=at_y(d),
            device_id_type=MESH,
        )
        copy.start()
        own.append(copy)

    wide[...] = jnp.zeros_like(wide)
    res[tiles] = jnp.zeros(res.shape[1:], res.dtype)
    occ_all[fit] = x_ref[...]

    def place(part, i, j):
        return (i * blocks + j if part == 0 else (fits // 2) * (blocks + j) + i) * 2 * FB

    def spread(part, wanted):
        def one(i, _):
            source = (fit - (2 * i + part) + fits) % fits
            for j in wanted:
                at = pl.multiple_of(place(part, i, j), 2 * FB)
                for o in range(occs):
                    piece = occ_all[source, j * FB : (j + 1) * FB, o * OB : (o + 1) * OB]
                    wide[o, pl.ds(at, FB), :OB] = piece
                    wide[o, pl.ds(at + FB, FB), OB:] = piece
            return 0

        lax.fori_loop(0, fits // 2, one, 0)

    def multiply(part, wanted, first, last):
        order = [(place(part, i, j), i, j) for i in range(fits // 2) for j in wanted]
        order.sort()
        start = order[0][0]

        def product(g):
            rows = []
            for u in range(GROUP):
                rows.append(jnp.concatenate(
                    [res[plan_ref[j * fits + 2 * i + part, g * GROUP + u]] for _, i, j in order], axis=1
                ))
            weights = wide[plan_ref[blocks * fits + 1, g], start : start + len(order) * 2 * FB, :]
            return jnp.dot(jnp.concatenate(rows, axis=0), weights, preferred_element_type=jnp.float32)

        def one(step, _):
            values = [product(step * TOGETHER + n) for n in range(TOGETHER)]
            height = AB // 2
            for n, value in enumerate(values):
                for u in range(GROUP):
                    parts = []
                    for k in range(NY):
                        at = u * height + k * 8
                        parts += [value[at : at + 8, :OB], value[at : at + 8, OB:]]
                    tile = jnp.concatenate(parts, axis=0)
                    slot = (step * TOGETHER + n) * GROUP + u
                    if part == 0:
                        acc[slot] = tile
                    else:
                        acc[slot] += tile
            return 0

        lax.fori_loop(first // TOGETHER, last // TOGETHER, one, 0)

    def pass_on(j):
        across[j].wait_recv()
        made = []
        for d in range(1, NY):
            copy = pltpu.make_async_remote_copy(
                src_ref=occ_all.at[partner, pl.ds(j * FB, FB)],
                dst_ref=occ_all.at[partner, pl.ds(j * FB, FB)],
                send_sem=send_fw.at[j, d - 1],
                recv_sem=recv_fw.at[j, d - 1],
                device_id=at_y(d),
                device_id_type=MESH,
            )
            copy.start()
            made.append(copy)
        return made

    for copy in own:
        copy.wait_recv()
    spread(0, range(blocks))
    fill.wait()
    all_groups = acc.shape[0] // GROUP
    multiply(0, range(blocks), 0, all_groups)
    forward = [pass_on(j) for j in range(blocks)]
    for made in forward:
        for copy in made:
            copy.wait_recv()
    spread(1, range(blocks))
    multiply(1, range(blocks), 0, all_groups)
    forward = [copy for made in forward for copy in made]

    per_block = NXC * CAP
    groups = per_block // 8

    def copies_y(i):
        made = []
        for d in range(1, NY):
            for n, (src, dst) in enumerate(((qy, ry), (sy, rsy))):
                made.append(pltpu.make_async_remote_copy(
                    src_ref=src.at[i, d - 1],
                    dst_ref=dst.at[i, d - 1],
                    send_sem=send_y.at[i, n, d - 1],
                    recv_sem=recv_y.at[i, n, d - 1],
                    device_id=at_y(d),
                    device_id_type=MESH,
                ))
        return made

    def copies_a(i, other):
        return [
            pltpu.make_async_remote_copy(
                src_ref=src.at[i, other],
                dst_ref=dst.at[i, zh],
                send_sem=send_a.at[i, n, other],
                recv_sem=recv_a.at[i, n, zh],
                device_id=at_z(i, other),
                device_id_type=MESH,
            )
            for n, (src, dst) in enumerate(((qa, ra), (sa, rsa)))
        ]

    def code(i):
        first = ((zl + offset(i)) % NZL) * per_block
        for d in range(1, NY):
            at = pl.multiple_of(((y + d) % NY) * 16, 16)
            for g in range(groups):
                values = jnp.concatenate(
                    [acc[plan_ref[blocks * fits, first + g * 8 + n], pl.ds(at, 16), :][None] for n in range(8)], axis=0
                )
                whole, scale = coded(values)
                qy[i, d - 1, g * 8 : g * 8 + 8] = whole
                sy[i, d - 1, g] = scale
        for copy in copies_y(i):
            copy.start()

    lower = lax.broadcasted_iota(jnp.int32, (8, OB), 0) < 4
    mine = pl.multiple_of(y * 16, 16)

    def collect(i):
        first = ((zl + offset(i)) % NZL) * per_block
        for copy in copies_y(i):
            copy.wait_recv()
        firsts, seconds = [], []
        for other in range(NXC):
            halves = ([], [])
            for rank in range(CAP):
                n = other * CAP + rank
                tile = acc[plan_ref[blocks * fits, first + n], pl.ds(mine, 16), :]
                for d in range(NY - 1):
                    tile = tile + decoded(ry[i, d, n]) * rsy[i, d, n // 8]
                a, b = tile[:8], tile[8:]
                halves[0].append(jnp.where(lower, a, pltpu.roll(b, 4, 0)))
                halves[1].append(jnp.where(lower, pltpu.roll(a, 4, 0), b))
            firsts.append(jnp.concatenate(halves[0], axis=0)[None])
            seconds.append(jnp.concatenate(halves[1], axis=0)[None])
        for k, values in enumerate((firsts, seconds)):
            whole, scale = coded(jnp.concatenate(values, axis=0))
            qa[i, k] = whole
            sa[i, k] = scale

    def send_on(i):
        for other in range(NZH):
            for copy in copies_a(i, other):
                copy.start()

    code(0)
    code(1)
    collect(0)
    first_a = copies_a(0, 1 - zh)
    for copy in first_a:
        copy.start()
    ra[0, zh] = qa[0, zh]
    rsa[0, zh] = sa[0, zh]

    def turn(i, _):
        code(i + 1)
        collect(i)
        send_on(i)
        return 0

    lax.fori_loop(1, NZL - 1, turn, 0)
    collect(NZL - 1)
    send_on(NZL - 1)

    def arrived(i, source):
        for n, dst in enumerate((ra, rsa)):
            pltpu.make_async_remote_copy(
                src_ref=dst.at[i, source],
                dst_ref=dst.at[i, source],
                send_sem=send_a.at[i, n, source],
                recv_sem=recv_a.at[i, n, source],
                device_id=at_z(i, source),
                device_id_type=MESH,
            ).wait_recv()

    def later(i, _):
        for source in range(NZH):
            arrived(i, source)
        return 0

    span = NZL // PARTS
    entries = NXC * span * NZH * CAP
    names = lax.broadcasted_iota(jnp.int32, (occs * OWN_CAP, entries), 0)
    copies_b = []

    def send_x(part):
        if part == 0:
            arrived(0, 1 - zh)
        lax.fori_loop(max(part * span, 1), (part + 1) * span, later, 0)
        here = pl.ds(part * span, span)
        made = []
        for d in range(1, NXC):
            other = (xc + d) % NXC
            for n, (src, dst) in enumerate((
                (ra.at[here, :, other], rb.at[part, xc]),
                (rsa.at[here], rsb.at[part, xc]),
            )):
                copy = pltpu.make_async_remote_copy(
                    src_ref=src,
                    dst_ref=dst,
                    send_sem=send_b.at[part, n, d - 1],
                    recv_sem=recv_b.at[part, n, d - 1],
                    device_id=at_x(d),
                    device_id_type=MESH,
                )
                copy.start()
                made.append(copy)
        for i in range(span):
            rb[part, xc, i] = ra[part * span + i, :, xc]
            rsb[part, xc, i] = rsa[part * span + i]
        copies_b.append(made)

    def add_up(part):
        for copy in copies_b[part]:
            copy.wait_recv()

        def expand(source, _):
            for i in range(span):
                for k in range(NZH):
                    value = decoded(rb[part, source, i, k]) * rsb[part, source, i, k]
                    flat[part, pl.ds(pl.multiple_of(((source * span + i) * NZH + k) * 16, 16), 16), :] = value
            return 0

        lax.fori_loop(0, NXC, expand, 0)
        select = (names == target_ref[part : part + 1, :]).astype(jnp.float32)
        for m in range(8):
            total = jnp.dot(
                select, flat[part, pl.ds(m, entries, stride=8), :],
                precision=lax.Precision.HIGHEST, preferred_element_type=jnp.float32,
            )
            if part:
                total += summed[m]
            if part + 1 < PARTS:
                summed[m] = total
                continue
            row = 2 * (m % 4) + m // 4
            for o in range(occs):
                final[o, pl.ds(row, OWN_CAP, stride=8), :] = total[o * OWN_CAP : (o + 1) * OWN_CAP]

    for part in range(PARTS):
        send_x(part)
        if part:
            add_up(part - 1)
    add_up(PARTS - 1)
    copies_b = [copy for made in copies_b for copy in made]
    for o in range(occs):
        out_ref[:, :, o * OB : (o + 1) * OB] = final[o].reshape(OWN_CAP, 8, OB).astype(out_ref.dtype)

    for copy in across + own + forward + copies_b + first_a:
        copy.wait_send()

    def sent_y(i, _):
        for copy in copies_y(i):
            copy.wait_send()
        return 0

    def sent_a(i, _):
        for other in range(NZH):
            for copy in copies_a(i, other):
                copy.wait_send()
        return 0

    lax.fori_loop(0, NZL, sent_y, 0)
    lax.fori_loop(1, NZL, sent_a, 0)


def exchange(plan, occ, rows, target):
    i16, f32, bf16 = jnp.int16, jnp.float32, jnp.bfloat16
    blocks, occs = occ.shape[0] // FB, occ.shape[1] // OB
    fits = NY * NZH
    slots = TILES + occs * GROUP
    dma = pltpu.SemaphoreType.DMA
    smem, vmem = pl.BlockSpec(memory_space=pltpu.SMEM), pl.BlockSpec(memory_space=pltpu.VMEM)
    return pl.pallas_call(
        exchange_kernel,
        out_shape=jax.ShapeDtypeStruct((OWN_CAP, AB // fits, occ.shape[1]), bf16),
        in_specs=[smem, vmem, pl.BlockSpec(memory_space=pl.ANY), vmem],
        out_specs=vmem,
        scratch_shapes=[
            pltpu.VMEM((fits,) + occ.shape, bf16),
            pltpu.VMEM((occs, fits * blocks * 2 * FB, 2 * OB), bf16),
            pltpu.VMEM((rows.shape[0] + 1,) + rows.shape[1:], bf16),
            pltpu.VMEM((slots, AB, OB), f32),
            pltpu.VMEM((NZL, NY - 1, NXC * CAP, 16, OB), i16),
            pltpu.VMEM((NZL, NY - 1, NXC * CAP // 8, 1, OB), f32),
            pltpu.VMEM((NZL, NY - 1, NXC * CAP, 16, OB), i16),
            pltpu.VMEM((NZL, NY - 1, NXC * CAP // 8, 1, OB), f32),
            pltpu.VMEM((NZL, NZH, NXC, 16, OB), i16),
            pltpu.VMEM((NZL, NZH, 1, OB), f32),
            pltpu.VMEM((NZL, NZH, NXC, 16, OB), i16),
            pltpu.VMEM((NZL, NZH, 1, OB), f32),
            pltpu.VMEM((PARTS, NXC, NZL // PARTS, NZH, 16, OB), i16),
            pltpu.VMEM((PARTS, NXC, NZL // PARTS, NZH, 1, OB), f32),
            pltpu.VMEM((PARTS, NXC * NZL // PARTS * NZH * 16, OB), f32),
            pltpu.VMEM((8, occs * OWN_CAP, OB), f32),
            pltpu.VMEM((occs, OWN_CAP * 8, OB), f32),
            dma((NY - 1,)), dma((NY - 1,)), dma((blocks,)), dma((blocks,)),
            dma((blocks, NY - 1)), dma((blocks, NY - 1)), dma,
            dma((NZL, 2, NY - 1)), dma((NZL, 2, NY - 1)),
            dma((NZL, 2, NZH)), dma((NZL, 2, NZH)),
            dma((PARTS, 2, NXC - 1)), dma((PARTS, 2, NXC - 1)),
        ],
        compiler_params=pltpu.CompilerParams(collective_id=0, has_side_effects=True, vmem_limit_bytes=48 << 20),
        name="exchange",
    )(plan, occ, rows, target)


def prepare_kernel(tiles_ref, pairs_ref, live_ref, list_ref, owner_ref, plan_ref, target_ref):
    f32, bf16 = jnp.float32, jnp.bfloat16
    ao = lax.axis_index("ao")
    zl = ao // NXC
    fits, width = tiles_ref.shape
    blocks = pairs_ref.shape[0]
    columns, tiles = list_ref.shape
    aos = owner_ref.shape[1]
    occs = OCCS
    slots = plan_ref.shape[1]
    none = fits * PAIRS

    def at(shape, axis):
        return lax.broadcasted_iota(jnp.int32, shape, axis)

    def dot(a, b):
        return jnp.dot(a.astype(bf16), b.astype(bf16), preferred_element_type=f32)

    def flip(a):
        n = a.shape[1]
        eye = (at((n, n), 0) == at((n, n), 1)).astype(bf16)
        return lax.dot_general(eye, a.astype(bf16), (((1,), (1,)), ((), ())), preferred_element_type=f32)

    def total(mask, value, axis):
        return jnp.sum(jnp.where(mask, value, 0.0), axis=axis, keepdims=True)

    codes = list_ref[pl.ds(ao, 1), :]
    eight = at((8, tiles), 0)
    both = jnp.where(eight == 0, codes & (occs - 1), codes >> OCC_BITS)
    turned = flip(both.astype(f32))
    occ_l = (codes & (occs - 1)).astype(f32)
    occ_s, block_s = turned[:, 0:1], turned[:, 1:2]
    row, lane = at((tiles, tiles), 0), at((tiles, tiles), 1)
    slot_l = total((occ_s == occ_l) & (row < lane), 1.0, 0)
    start = jnp.zeros((1, 1), f32)
    groups = at((1, slots), 1) * GROUP
    group_occ = jnp.zeros((1, slots), f32)
    for o in range(occs):
        slot_l = slot_l + jnp.where(occ_l == o, start, 0.0)
        if o:
            group_occ = group_occ + jnp.where(groups.astype(f32) >= start, 1.0, 0.0)
        count = total(occ_l == o, 1.0, 1)
        start = start + jnp.floor((count + (GROUP - 1)) * (1.0 / GROUP)) * GROUP

    owner_row = owner_ref[...].astype(f32)
    where_s = total(block_s == at((tiles, aos), 1).astype(f32), owner_row, 1)
    owner_s = jnp.floor(where_s * (1.0 / OWN_CAP))
    eye = row == lane
    owner_l = total(eye, owner_s, 0)
    slot_s = total(eye, slot_l, 1)
    place_l = owner_l * CAP + total((owner_s == owner_l) & (row < lane), 1.0, 0)
    place_s = total(eye, place_l, 1)
    wide = at((tiles, slots), 1).astype(f32)
    index = total(place_s == wide, slot_s, 0)

    live_s = total(at((fits, fits), 0) == at((fits, fits), 1), live_ref[...].astype(f32), 1)
    inside = at((fits, width), 1).astype(f32) < live_s
    values = []
    for j in range(blocks):
        pair = pairs_ref[j]
        value = (pair + at((fits, width), 0) * PAIRS - none).astype(f32)
        values.append(jnp.where((pair.astype(f32) >= 0.0) & inside, value, 0.0))
    values = jnp.concatenate(values, axis=0)
    rows_s = flip(tiles_ref[...].astype(f32))
    step_of = at(values.shape, 0) % fits
    by_tile = jnp.zeros((values.shape[0], tiles), f32)
    for s in range(fits):
        hit = (rows_s[:, s : s + 1] == at((width, tiles), 1).astype(f32)).astype(f32)
        by_tile = by_tile + jnp.where(step_of == s, dot(values, hit), 0.0)
    table = dot(by_tile, (slot_s == wide).astype(f32)) + none
    high = values.shape[0]
    plan_ref[0:high, :] = table.astype(jnp.int32)
    last = at((8, slots), 0)
    extra = jnp.where(last == 0, index, jnp.where(last == 1, group_occ, 0.0))
    plan_ref[high : high + 8, :] = extra.astype(jnp.int32)

    mine = (ao * OWN_CAP + at((OWN_CAP, aos), 0)).astype(f32)
    held = total(owner_row == mine, (at((OWN_CAP, aos), 1) + 1).astype(f32), 1) - 1.0
    listed = list_ref[...]
    names = (listed >> OCC_BITS).astype(f32)
    place = jnp.full(names.shape, -1.0, f32)
    for i in range(OWN_CAP):
        place = jnp.where(names == held[i : i + 1, :], float(i), place)
    owned = place >= 0.0
    goal = (listed & (occs - 1)).astype(f32) * OWN_CAP + place
    rank = dot(jnp.where(owned, 1.0, 0.0), (row < lane).astype(f32))
    goals = [total(owned & (rank == r), goal + 1.0, 1) for r in range(CAP)]
    span = NZL // PARTS
    entry = at((columns, target_ref.shape[1]), 1)
    column = at((columns, target_ref.shape[1]), 0)
    rank_of, turn = entry % CAP, entry // (CAP * NZH) % span
    side = entry // (CAP * NZH * span)
    for part in range(PARTS):
        k = part * span + turn
        source = (zl - offset(k) + NZL) % NZL * NXC + side
        goal_of = jnp.where(rank_of == 0, goals[0], goals[1])
        target_ref[part : part + 1, :] = (total(column == source, goal_of, 0) - 1.0).astype(jnp.int32)


def prepare(row_tiles, row_pairs, live_rows, tile_list, owner_slot):
    blocks, fits, width = row_pairs.shape
    vmem = pl.BlockSpec(memory_space=pltpu.VMEM)
    return pl.pallas_call(
        prepare_kernel,
        out_shape=[
            jax.ShapeDtypeStruct((blocks * fits + 8, 128), jnp.int32),
            jax.ShapeDtypeStruct((PARTS, NXC * NZL // PARTS * NZH * CAP), jnp.int32),
        ],
        in_specs=[vmem] * 5,
        out_specs=[vmem] * 2,
        name="prepare",
    )(row_tiles, row_pairs, live_rows, tile_list, owner_slot.reshape(1, -1))


def shards(occ_blocks, resident, row_tiles, row_pairs, live_rows, tile_list, owner_slot):
    plan, target = prepare(row_tiles[0], row_pairs[:, 0], live_rows, tile_list, owner_slot)
    rows = resident.reshape(resident.shape[0], AB // 2, 2 * FB)
    return exchange(plan, occ_blocks, rows, target)


def solution(mesh):
    return jax.shard_map(
        shards,
        mesh=mesh,
        in_specs=(
            P(("fit", "ao"), None),
            P(("fit", "ao"), None),
            P(("fit", "ao"), None, None),
            P(None, ("fit", "ao"), None, None),
            P(("fit", "ao"), None),
            P(),
            P(),
        ),
        out_specs=P("ao", "fit", None),
        check_vma=False,
    )
```

```python
import functools

import jax
import jax.numpy as jnp
from jax import lax
from jax.experimental import pallas as pl
from jax.experimental.pallas import tpu as pltpu
from jax.sharding import PartitionSpec as P

AB = 64
FB = 64
OB = 128
OWN_CAP = 8
CAP = 2
NY = 4
NZH = 2
NZL = 8
NXC = 8
GROUP = 4
PARTS = 4
TOGETHER = 7
TILES = 96
OCCS = 4
OCC_BITS = 2
PAIRS = 32
MESH = pl.DeviceIdType.MESH
TOP = 32767.0
TINY = 1e-30


def offset(k):
    odd = k % 2
    return odd * ((k + 1) // 2) + (1 - odd) * ((NZL - k // 2) % NZL)


def coded(values):
    top = jnp.maximum(jnp.max(jnp.max(jnp.abs(values), axis=0), axis=0, keepdims=True), TINY)
    whole = jnp.round(values * (TOP / top)[None])
    return whole.astype(jnp.int32).astype(jnp.int16), top * (1.0 / TOP)


def decoded(whole):
    return whole.astype(jnp.int32).astype(jnp.float32)


def exchange_kernel(
    plan_in, x_ref, res_ref, target_in, out_ref,
    plan_ref, target_ref, occ_all, wide, raw, res, acc, qy, sy, ry, rsy, qa, sa, ra, rsa, rb, rsb, flat, summed, final,
    send_own, recv_own, send_z, recv_z, send_fw, recv_fw, local_sem, plan_sem, target_sem, own_sem,
    send_y, recv_y, send_a, recv_a, send_b, recv_b,
):
    fit = lax.axis_index("fit")
    ao = lax.axis_index("ao")
    y, zh = fit // NZH, fit % NZH
    zl, xc = ao // NXC, ao % NXC
    fits = NY * NZH
    partner = y * NZH + (1 - zh)
    blocks = x_ref.shape[0] // FB
    occs = out_ref.shape[2] // OB
    tiles = res_ref.shape[0]
    per_step = tiles // fits
    half = wide.shape[1] // 2

    def at_y(d):
        return (((y + d) % NY) * NZH + zh, ao)

    def at_z(i, other):
        return (y * NZH + other, ((zl + offset(i)) % NZL) * NXC + xc)

    def at_x(d):
        return (fit, zl * NXC + (xc + d) % NXC)

    fill = pltpu.make_async_copy(res_ref, raw, local_sem)
    fill.start()
    plan_copy = pltpu.make_async_copy(plan_in, plan_ref, plan_sem)
    plan_copy.start()
    target_copy = pltpu.make_async_copy(target_in, target_ref, target_sem)
    target_copy.start()
    own_copy = pltpu.make_async_copy(x_ref, occ_all.at[fit], own_sem)
    own_copy.start()
    barrier = pltpu.get_barrier_semaphore()
    pl.semaphore_signal(barrier, inc=1, device_id=(partner, ao), device_id_type=MESH)
    for d in range(1, NY):
        pl.semaphore_signal(barrier, inc=1, device_id=at_y(d), device_id_type=MESH)
    for i in range(1, NZL):
        for other in range(NZH):
            pl.semaphore_signal(barrier, inc=1, device_id=at_z(i, other), device_id_type=MESH)
    for d in range(1, NXC):
        pl.semaphore_signal(barrier, inc=1, device_id=at_x(d), device_id_type=MESH)
    pl.semaphore_wait(barrier, NY + (NZL - 1) * NZH + NXC - 1)

    across = []
    for j in range(blocks):
        copy = pltpu.make_async_remote_copy(
            src_ref=x_ref.at[pl.ds(j * FB, FB)],
            dst_ref=occ_all.at[fit, pl.ds(j * FB, FB)],
            send_sem=send_z.at[j],
            recv_sem=recv_z.at[j],
            device_id=(partner, ao),
            device_id_type=MESH,
        )
        copy.start()
        across.append(copy)
    own = []
    for d in range(1, NY):
        copy = pltpu.make_async_remote_copy(
            src_ref=x_ref,
            dst_ref=occ_all.at[fit],
            send_sem=send_own.at[d - 1],
            recv_sem=recv_own.at[d - 1],
            device_id=at_y(d),
            device_id_type=MESH,
        )
        copy.start()
        own.append(copy)

    wide[...] = jnp.zeros_like(wide)
    res[tiles] = jnp.zeros(res.shape[1:], res.dtype)
    fill.wait()

    def lay(s, _):
        at = pl.multiple_of(s * 16, 16)
        pieces = [raw[pl.ds(at, 16), m * OB : (m + 1) * OB] for m in range(AB // 2)]
        res[pl.ds(at, 16)] = jnp.swapaxes(jnp.stack(pieces, axis=0), 0, 1)
        return 0

    lax.fori_loop(0, tiles // 16, lay, 0)

    def place(part, i, j):
        return (i * blocks + j if part == 0 else (fits // 2) * (blocks + j) + i) * 2 * FB

    def spread(part, wanted):
        def one(i, _):
            source = (fit - (2 * i + part) + fits) % fits
            for j in wanted:
                at = pl.multiple_of(place(part, i, j), 2 * FB)
                for o in range(occs):
                    piece = occ_all[source, j * FB : (j + 1) * FB, o * OB : (o + 1) * OB]
                    wide[o, pl.ds(at, FB), :OB] = piece
                    wide[o, pl.ds(at + FB, FB), OB:] = piece
            return 0

        lax.fori_loop(0, fits // 2, one, 0)

    def multiply(part, wanted, first, last):
        order = [(place(part, i, j), i, j) for i in range(fits // 2) for j in wanted]
        order.sort()
        start = order[0][0]

        def product(g):
            rows = []
            for u in range(GROUP):
                rows.append(jnp.concatenate(
                    [res[plan_ref[j * fits + 2 * i + part, g * GROUP + u]] for _, i, j in order], axis=1
                ))
            weights = wide[plan_ref[blocks * fits + 1, g], start : start + len(order) * 2 * FB, :]
            return jnp.dot(jnp.concatenate(rows, axis=0), weights, preferred_element_type=jnp.float32)

        def one(step, _):
            values = [product(step * TOGETHER + n) for n in range(TOGETHER)]
            height = AB // 2
            for n, value in enumerate(values):
                for u in range(GROUP):
                    parts = []
                    for k in range(NY):
                        at = u * height + k * 8
                        parts += [value[at : at + 8, :OB], value[at : at + 8, OB:]]
                    tile = jnp.concatenate(parts, axis=0)
                    slot = (step * TOGETHER + n) * GROUP + u
                    if part == 0:
                        acc[slot] = tile
                    else:
                        acc[slot] += tile
            return 0

        lax.fori_loop(first // TOGETHER, last // TOGETHER, one, 0)

    def pass_on(j):
        across[j].wait_recv()
        made = []
        for d in range(1, NY):
            copy = pltpu.make_async_remote_copy(
                src_ref=occ_all.at[partner, pl.ds(j * FB, FB)],
                dst_ref=occ_all.at[partner, pl.ds(j * FB, FB)],
                send_sem=send_fw.at[j, d - 1],
                recv_sem=recv_fw.at[j, d - 1],
                device_id=at_y(d),
                device_id_type=MESH,
            )
            copy.start()
            made.append(copy)
        return made

    for copy in own:
        copy.wait_recv()
    own_copy.wait()
    spread(0, range(blocks))
    plan_copy.wait()
    target_copy.wait()
    all_groups = acc.shape[0] // GROUP
    multiply(0, range(blocks), 0, all_groups)
    forward = []
    for j in range(blocks + 1):
        if j < blocks:
            forward.append(pass_on(j))
        if j:
            for copy in forward[j - 1]:
                copy.wait_recv()
            spread(1, [j - 1])
    multiply(1, range(blocks), 0, all_groups)
    forward = [copy for made in forward for copy in made]

    per_block = NXC * CAP
    groups = per_block // 8

    def copies_y(i):
        made = []
        for d in range(1, NY):
            for n, (src, dst) in enumerate(((qy, ry), (sy, rsy))):
                made.append(pltpu.make_async_remote_copy(
                    src_ref=src.at[i, d - 1],
                    dst_ref=dst.at[i, d - 1],
                    send_sem=send_y.at[i, n, d - 1],
                    recv_sem=recv_y.at[i, n, d - 1],
                    device_id=at_y(d),
                    device_id_type=MESH,
                ))
        return made

    def copies_a(i, other):
        return [
            pltpu.make_async_remote_copy(
                src_ref=src.at[i, other],
                dst_ref=dst.at[i, zh],
                send_sem=send_a.at[i, n, other],
                recv_sem=recv_a.at[i, n, zh],
                device_id=at_z(i, other),
                device_id_type=MESH,
            )
            for n, (src, dst) in enumerate(((qa, ra), (sa, rsa)))
        ]

    def code(i):
        first = ((zl + offset(i)) % NZL) * per_block
        for d in range(1, NY):
            at = pl.multiple_of(((y + d) % NY) * 16, 16)
            for g in range(groups):
                values = jnp.concatenate(
                    [acc[plan_ref[blocks * fits, first + g * 8 + n], pl.ds(at, 16), :][None] for n in range(8)], axis=0
                )
                whole, scale = coded(values)
                qy[i, d - 1, g * 8 : g * 8 + 8] = whole
                sy[i, d - 1, g] = scale
        for copy in copies_y(i):
            copy.start()

    lower = lax.broadcasted_iota(jnp.int32, (8, OB), 0) < 4
    mine = pl.multiple_of(y * 16, 16)

    def collect(i):
        first = ((zl + offset(i)) % NZL) * per_block
        for copy in copies_y(i):
            copy.wait_recv()
        firsts, seconds = [], []
        for other in range(NXC):
            halves = ([], [])
            for rank in range(CAP):
                n = other * CAP + rank
                tile = acc[plan_ref[blocks * fits, first + n], pl.ds(mine, 16), :]
                for d in range(NY - 1):
                    tile = tile + decoded(ry[i, d, n]) * rsy[i, d, n // 8]
                a, b = tile[:8], tile[8:]
                halves[0].append(jnp.where(lower, a, pltpu.roll(b, 4, 0)))
                halves[1].append(jnp.where(lower, pltpu.roll(a, 4, 0), b))
            firsts.append(jnp.concatenate(halves[0], axis=0)[None])
            seconds.append(jnp.concatenate(halves[1], axis=0)[None])
        for k, values in enumerate((firsts, seconds)):
            whole, scale = coded(jnp.concatenate(values, axis=0))
            qa[i, k] = whole
            sa[i, k] = scale

    def send_on(i):
        for other in range(NZH):
            for copy in copies_a(i, other):
                copy.start()

    def code_one(i, _):
        code(i)
        return 0

    lax.fori_loop(0, NZL, code_one, 0)
    collect(0)
    first_a = copies_a(0, 1 - zh)
    for copy in first_a:
        copy.start()
    ra[0, zh] = qa[0, zh]
    rsa[0, zh] = sa[0, zh]

    def turn(i, _):
        collect(i)
        send_on(i)
        return 0

    lax.fori_loop(1, NZL - 1, turn, 0)
    collect(NZL - 1)
    send_on(NZL - 1)

    def arrived(i, source):
        for n, dst in enumerate((ra, rsa)):
            pltpu.make_async_remote_copy(
                src_ref=dst.at[i, source],
                dst_ref=dst.at[i, source],
                send_sem=send_a.at[i, n, source],
                recv_sem=recv_a.at[i, n, source],
                device_id=at_z(i, source),
                device_id_type=MESH,
            ).wait_recv()

    def later(i, _):
        for source in range(NZH):
            arrived(i, source)
        return 0

    span = NZL // PARTS
    entries = NXC * span * NZH * CAP
    names = lax.broadcasted_iota(jnp.int32, (occs * OWN_CAP, entries), 0)
    copies_b = []

    def send_x(part):
        if part == 0:
            arrived(0, 1 - zh)
        lax.fori_loop(max(part * span, 1), (part + 1) * span, later, 0)
        here = pl.ds(part * span, span)
        made = []
        for d in range(1, NXC):
            other = (xc + d) % NXC
            for n, (src, dst) in enumerate((
                (ra.at[here, :, other], rb.at[part, xc]),
                (rsa.at[here], rsb.at[part, xc]),
            )):
                copy = pltpu.make_async_remote_copy(
                    src_ref=src,
                    dst_ref=dst,
                    send_sem=send_b.at[part, n, d - 1],
                    recv_sem=recv_b.at[part, n, d - 1],
                    device_id=at_x(d),
                    device_id_type=MESH,
                )
                copy.start()
                made.append(copy)
        for i in range(span):
            rb[part, xc, i] = ra[part * span + i, :, xc]
            rsb[part, xc, i] = rsa[part * span + i]
        copies_b.append(made)

    def add_up(part):
        for copy in copies_b[part]:
            copy.wait_recv()

        def expand(source, _):
            for i in range(span):
                for k in range(NZH):
                    value = decoded(rb[part, source, i, k]) * rsb[part, source, i, k]
                    flat[part, pl.ds(pl.multiple_of(((source * span + i) * NZH + k) * 16, 16), 16), :] = value
            return 0

        lax.fori_loop(0, NXC, expand, 0)
        select = (names == target_ref[part : part + 1, :]).astype(jnp.float32)
        for m in range(8):
            total = jnp.dot(
                select, flat[part, pl.ds(m, entries, stride=8), :],
                precision=lax.Precision.HIGHEST, preferred_element_type=jnp.float32,
            )
            if part:
                total += summed[m]
            if part + 1 < PARTS:
                summed[m] = total
                continue
            row = 2 * (m % 4) + m // 4
            for o in range(occs):
                final[o, pl.ds(row, OWN_CAP, stride=8), :] = total[o * OWN_CAP : (o + 1) * OWN_CAP]

    for part in range(PARTS):
        send_x(part)
        if part:
            add_up(part - 1)
    add_up(PARTS - 1)
    copies_b = [copy for made in copies_b for copy in made]
    for o in range(occs):
        out_ref[:, :, o * OB : (o + 1) * OB] = final[o].reshape(OWN_CAP, 8, OB).astype(out_ref.dtype)

    for copy in across + own + forward + copies_b + first_a:
        copy.wait_send()

    def sent_y(i, _):
        for copy in copies_y(i):
            copy.wait_send()
        return 0

    def sent_a(i, _):
        for other in range(NZH):
            for copy in copies_a(i, other):
                copy.wait_send()
        return 0

    lax.fori_loop(0, NZL, sent_y, 0)
    lax.fori_loop(1, NZL, sent_a, 0)


def exchange(plan, occ, rows, target):
    i16, f32, bf16 = jnp.int16, jnp.float32, jnp.bfloat16
    blocks, occs = occ.shape[0] // FB, occ.shape[1] // OB
    fits = NY * NZH
    slots = TILES + occs * GROUP
    dma = pltpu.SemaphoreType.DMA
    vmem = pl.BlockSpec(memory_space=pltpu.VMEM)
    return pl.pallas_call(
        exchange_kernel,
        out_shape=jax.ShapeDtypeStruct((OWN_CAP, AB // fits, occ.shape[1]), bf16),
        in_specs=[pl.BlockSpec(memory_space=pltpu.HBM)] * 4,
        out_specs=vmem,
        scratch_shapes=[
            pltpu.SMEM(plan.shape, jnp.int32),
            pltpu.VMEM(target.shape, jnp.int32),
            pltpu.VMEM((fits,) + occ.shape, bf16),
            pltpu.VMEM((occs, fits * blocks * 2 * FB, 2 * OB), bf16),
            pltpu.VMEM(rows.shape, bf16),
            pltpu.VMEM((rows.shape[0] + 1, AB // 2, 2 * FB), bf16),
            pltpu.VMEM((slots, AB, OB), f32),
            pltpu.VMEM((NZL, NY - 1, NXC * CAP, 16, OB), i16),
            pltpu.VMEM((NZL, NY - 1, NXC * CAP // 8, 1, OB), f32),
            pltpu.VMEM((NZL, NY - 1, NXC * CAP, 16, OB), i16),
            pltpu.VMEM((NZL, NY - 1, NXC * CAP // 8, 1, OB), f32),
            pltpu.VMEM((NZL, NZH, NXC, 16, OB), i16),
            pltpu.VMEM((NZL, NZH, 1, OB), f32),
            pltpu.VMEM((NZL, NZH, NXC, 16, OB), i16),
            pltpu.VMEM((NZL, NZH, 1, OB), f32),
            pltpu.VMEM((PARTS, NXC, NZL // PARTS, NZH, 16, OB), i16),
            pltpu.VMEM((PARTS, NXC, NZL // PARTS, NZH, 1, OB), f32),
            pltpu.VMEM((PARTS, NXC * NZL // PARTS * NZH * 16, OB), f32),
            pltpu.VMEM((8, occs * OWN_CAP, OB), f32),
            pltpu.VMEM((occs, OWN_CAP * 8, OB), f32),
            dma((NY - 1,)), dma((NY - 1,)), dma((blocks,)), dma((blocks,)),
            dma((blocks, NY - 1)), dma((blocks, NY - 1)), dma, dma, dma, dma,
            dma((NZL, 2, NY - 1)), dma((NZL, 2, NY - 1)),
            dma((NZL, 2, NZH)), dma((NZL, 2, NZH)),
            dma((PARTS, 2, NXC - 1)), dma((PARTS, 2, NXC - 1)),
        ],
        compiler_params=pltpu.CompilerParams(collective_id=0, has_side_effects=True, vmem_limit_bytes=58 << 20),
        name="exchange",
    )(plan, occ, rows, target)


def prepare_kernel(tiles_ref, pairs_ref, live_ref, list_ref, owner_ref, plan_ref, target_ref):
    f32, bf16 = jnp.float32, jnp.bfloat16
    ao = lax.axis_index("ao")
    zl = ao // NXC
    fits, width = tiles_ref.shape
    blocks = pairs_ref.shape[0]
    columns, tiles = list_ref.shape
    aos = owner_ref.shape[1]
    occs = OCCS
    slots = plan_ref.shape[1]
    none = fits * PAIRS

    def at(shape, axis):
        return lax.broadcasted_iota(jnp.int32, shape, axis)

    def dot(a, b):
        return jnp.dot(a.astype(bf16), b.astype(bf16), preferred_element_type=f32)

    def flip(a):
        n = a.shape[1]
        eye = (at((n, n), 0) == at((n, n), 1)).astype(bf16)
        return lax.dot_general(eye, a.astype(bf16), (((1,), (1,)), ((), ())), preferred_element_type=f32)

    def total(mask, value, axis):
        return jnp.sum(jnp.where(mask, value, 0.0), axis=axis, keepdims=True)

    codes = list_ref[pl.ds(ao, 1), :]
    eight = at((8, tiles), 0)
    both = jnp.where(eight == 0, codes & (occs - 1), codes >> OCC_BITS)
    turned = flip(both.astype(f32))
    occ_l = (codes & (occs - 1)).astype(f32)
    occ_s, block_s = turned[:, 0:1], turned[:, 1:2]
    row, lane = at((tiles, tiles), 0), at((tiles, tiles), 1)
    slot_l = total((occ_s == occ_l) & (row < lane), 1.0, 0)
    start = jnp.zeros((1, 1), f32)
    groups = at((1, slots), 1) * GROUP
    group_occ = jnp.zeros((1, slots), f32)
    for o in range(occs):
        slot_l = slot_l + jnp.where(occ_l == o, start, 0.0)
        if o:
            group_occ = group_occ + jnp.where(groups.astype(f32) >= start, 1.0, 0.0)
        count = total(occ_l == o, 1.0, 1)
        start = start + jnp.floor((count + (GROUP - 1)) * (1.0 / GROUP)) * GROUP

    owner_row = owner_ref[...].astype(f32)
    where_s = total(block_s == at((tiles, aos), 1).astype(f32), owner_row, 1)
    owner_s = jnp.floor(where_s * (1.0 / OWN_CAP))
    eye = row == lane
    owner_l = total(eye, owner_s, 0)
    slot_s = total(eye, slot_l, 1)
    place_l = owner_l * CAP + total((owner_s == owner_l) & (row < lane), 1.0, 0)
    place_s = total(eye, place_l, 1)
    wide = at((tiles, slots), 1).astype(f32)
    index = total(place_s == wide, slot_s, 0)

    live_s = total(at((fits, fits), 0) == at((fits, fits), 1), live_ref[...].astype(f32), 1)
    inside = at((fits, width), 1).astype(f32) < live_s
    values = []
    for j in range(blocks):
        pair = pairs_ref[j]
        value = (pair + at((fits, width), 0) * PAIRS - none).astype(f32)
        values.append(jnp.where((pair.astype(f32) >= 0.0) & inside, value, 0.0))
    values = jnp.concatenate(values, axis=0)
    rows_s = flip(tiles_ref[...].astype(f32))
    step_of = at(values.shape, 0) % fits
    by_tile = jnp.zeros((values.shape[0], tiles), f32)
    for s in range(fits):
        hit = (rows_s[:, s : s + 1] == at((width, tiles), 1).astype(f32)).astype(f32)
        by_tile = by_tile + jnp.where(step_of == s, dot(values, hit), 0.0)
    table = dot(by_tile, (slot_s == wide).astype(f32)) + none
    high = values.shape[0]
    plan_ref[0:high, :] = table.astype(jnp.int32)
    last = at((8, slots), 0)
    extra = jnp.where(last == 0, index, jnp.where(last == 1, group_occ, 0.0))
    plan_ref[high : high + 8, :] = extra.astype(jnp.int32)

    mine = (ao * OWN_CAP + at((OWN_CAP, aos), 0)).astype(f32)
    held = total(owner_row == mine, (at((OWN_CAP, aos), 1) + 1).astype(f32), 1) - 1.0
    listed = list_ref[...]
    names = (listed >> OCC_BITS).astype(f32)
    place = jnp.full(names.shape, -1.0, f32)
    for i in range(OWN_CAP):
        place = jnp.where(names == held[i : i + 1, :], float(i), place)
    owned = place >= 0.0
    goal = (listed & (occs - 1)).astype(f32) * OWN_CAP + place
    rank = dot(jnp.where(owned, 1.0, 0.0), (row < lane).astype(f32))
    goals = [total(owned & (rank == r), goal + 1.0, 1) for r in range(CAP)]
    span = NZL // PARTS
    entry = at((columns, target_ref.shape[1]), 1)
    column = at((columns, target_ref.shape[1]), 0)
    rank_of, turn = entry % CAP, entry // (CAP * NZH) % span
    side = entry // (CAP * NZH * span)
    for part in range(PARTS):
        k = part * span + turn
        source = (zl - offset(k) + NZL) % NZL * NXC + side
        goal_of = jnp.where(rank_of == 0, goals[0], goals[1])
        target_ref[part : part + 1, :] = (total(column == source, goal_of, 0) - 1.0).astype(jnp.int32)


def prepare(row_tiles, row_pairs, live_rows, tile_list, owner_slot):
    blocks, fits, width = row_pairs.shape
    vmem = pl.BlockSpec(memory_space=pltpu.VMEM)
    return pl.pallas_call(
        prepare_kernel,
        out_shape=[
            jax.ShapeDtypeStruct((blocks * fits + 8, 128), jnp.int32),
            jax.ShapeDtypeStruct((PARTS, NXC * NZL // PARTS * NZH * CAP), jnp.int32),
        ],
        in_specs=[vmem] * 5,
        out_specs=[vmem] * 2,
        name="prepare",
    )(row_tiles, row_pairs, live_rows, tile_list, owner_slot.reshape(1, -1))


def shards(occ_blocks, resident, row_tiles, row_pairs, live_rows, tile_list, owner_slot):
    plan, target = prepare(row_tiles[0], row_pairs[:, 0], live_rows, tile_list, owner_slot)
    return exchange(plan, occ_blocks, resident, target)


def solution(mesh):
    return jax.shard_map(
        shards,
        mesh=mesh,
        in_specs=(
            P(("fit", "ao"), None),
            P(("fit", "ao"), None),
            P(("fit", "ao"), None, None),
            P(None, ("fit", "ao"), None, None),
            P(("fit", "ao"), None),
            P(),
            P(),
        ),
        out_specs=P("ao", "fit", None),
        check_vma=False,
    )
```

```python
import functools

import jax
import jax.numpy as jnp
from jax import lax
from jax.experimental import pallas as pl
from jax.experimental.pallas import tpu as pltpu
from jax.sharding import PartitionSpec as P

AB = 64
FB = 64
OB = 128
OWN_CAP = 8
CAP = 2
NY = 4
NZH = 2
NZL = 8
NXC = 8
GROUP = 4
PARTS = 4
TOGETHER = 7
TILES = 96
OCCS = 4
OCC_BITS = 2
PAIRS = 32
MESH = pl.DeviceIdType.MESH
TOP = 32767.0
TINY = 1e-30


def offset(k):
    odd = k % 2
    return odd * ((k + 1) // 2) + (1 - odd) * ((NZL - k // 2) % NZL)


def coded(values):
    top = jnp.maximum(jnp.max(jnp.max(jnp.abs(values), axis=0), axis=0, keepdims=True), TINY)
    whole = jnp.round(values * (TOP / top)[None])
    return whole.astype(jnp.int32).astype(jnp.int16), top * (1.0 / TOP)


def decoded(whole):
    return whole.astype(jnp.int32).astype(jnp.float32)


def exchange_kernel(
    tiles_in, pairs_in, live_in, list_in, owner_in, x_ref, res_ref, out_ref,
    tiles_ref, pairs_ref, live_ref, list_ref, owner_ref, plan_made, plan_ref, target_ref, occ_all, wide, raw, res, acc, qy, sy, ry, rsy, qa, sa, ra, rsa, rb, rsb, flat, summed, final,
    send_own, recv_own, send_z, recv_z, send_fw, recv_fw, local_sem, plan_sem, table_sem, own_sem,
    send_y, recv_y, send_a, recv_a, send_b, recv_b,
):
    fit = lax.axis_index("fit")
    ao = lax.axis_index("ao")
    y, zh = fit // NZH, fit % NZH
    zl, xc = ao // NXC, ao % NXC
    fits = NY * NZH
    partner = y * NZH + (1 - zh)
    blocks = x_ref.shape[0] // FB
    occs = out_ref.shape[2] // OB
    tiles = res_ref.shape[0]
    per_step = tiles // fits
    half = wide.shape[1] // 2

    def at_y(d):
        return (((y + d) % NY) * NZH + zh, ao)

    def at_z(i, other):
        return (y * NZH + other, ((zl + offset(i)) % NZL) * NXC + xc)

    def at_x(d):
        return (fit, zl * NXC + (xc + d) % NXC)

    fill = pltpu.make_async_copy(res_ref, raw, local_sem)
    fill.start()
    pairs = ((tiles_in, tiles_ref), (pairs_in, pairs_ref), (live_in, live_ref), (list_in, list_ref), (owner_in, owner_ref))
    tables = [pltpu.make_async_copy(src, dst, table_sem.at[n]) for n, (src, dst) in enumerate(pairs)]
    for copy in tables:
        copy.start()
    own_copy = pltpu.make_async_copy(x_ref, occ_all.at[fit], own_sem)
    own_copy.start()
    barrier = pltpu.get_barrier_semaphore()
    pl.semaphore_signal(barrier, inc=1, device_id=(partner, ao), device_id_type=MESH)
    for d in range(1, NY):
        pl.semaphore_signal(barrier, inc=1, device_id=at_y(d), device_id_type=MESH)
    for i in range(1, NZL):
        for other in range(NZH):
            pl.semaphore_signal(barrier, inc=1, device_id=at_z(i, other), device_id_type=MESH)
    for d in range(1, NXC):
        pl.semaphore_signal(barrier, inc=1, device_id=at_x(d), device_id_type=MESH)
    pl.semaphore_wait(barrier, NY + (NZL - 1) * NZH + NXC - 1)

    across = []
    for j in range(blocks):
        copy = pltpu.make_async_remote_copy(
            src_ref=x_ref.at[pl.ds(j * FB, FB)],
            dst_ref=occ_all.at[fit, pl.ds(j * FB, FB)],
            send_sem=send_z.at[j],
            recv_sem=recv_z.at[j],
            device_id=(partner, ao),
            device_id_type=MESH,
        )
        copy.start()
        across.append(copy)
    own = []
    for d in range(1, NY):
        copy = pltpu.make_async_remote_copy(
            src_ref=x_ref,
            dst_ref=occ_all.at[fit],
            send_sem=send_own.at[d - 1],
            recv_sem=recv_own.at[d - 1],
            device_id=at_y(d),
            device_id_type=MESH,
        )
        copy.start()
        own.append(copy)

    wide[...] = jnp.zeros_like(wide)
    res[tiles] = jnp.zeros(res.shape[1:], res.dtype)
    fill.wait()

    def lay(s, _):
        at = pl.multiple_of(s * 16, 16)
        pieces = [raw[pl.ds(at, 16), m * OB : (m + 1) * OB] for m in range(AB // 2)]
        res[pl.ds(at, 16)] = jnp.swapaxes(jnp.stack(pieces, axis=0), 0, 1)
        return 0

    lax.fori_loop(0, tiles // 16, lay, 0)

    def place(part, i, j):
        return (i * blocks + j if part == 0 else (fits // 2) * (blocks + j) + i) * 2 * FB

    def spread(part, wanted):
        def one(i, _):
            source = (fit - (2 * i + part) + fits) % fits
            for j in wanted:
                at = pl.multiple_of(place(part, i, j), 2 * FB)
                for o in range(occs):
                    piece = occ_all[source, j * FB : (j + 1) * FB, o * OB : (o + 1) * OB]
                    wide[o, pl.ds(at, FB), :OB] = piece
                    wide[o, pl.ds(at + FB, FB), OB:] = piece
            return 0

        lax.fori_loop(0, fits // 2, one, 0)

    def multiply(part, wanted, first, last):
        order = [(place(part, i, j), i, j) for i in range(fits // 2) for j in wanted]
        order.sort()
        start = order[0][0]

        def product(g):
            rows = []
            for u in range(GROUP):
                rows.append(jnp.concatenate(
                    [res[plan_ref[j * fits + 2 * i + part, g * GROUP + u]] for _, i, j in order], axis=1
                ))
            weights = wide[plan_ref[blocks * fits + 1, g], start : start + len(order) * 2 * FB, :]
            return jnp.dot(jnp.concatenate(rows, axis=0), weights, preferred_element_type=jnp.float32)

        def one(step, _):
            values = [product(step * TOGETHER + n) for n in range(TOGETHER)]
            height = AB // 2
            for n, value in enumerate(values):
                for u in range(GROUP):
                    parts = []
                    for k in range(NY):
                        at = u * height + k * 8
                        parts += [value[at : at + 8, :OB], value[at : at + 8, OB:]]
                    tile = jnp.concatenate(parts, axis=0)
                    slot = (step * TOGETHER + n) * GROUP + u
                    if part == 0:
                        acc[slot] = tile
                    else:
                        acc[slot] += tile
            return 0

        lax.fori_loop(first // TOGETHER, last // TOGETHER, one, 0)

    def pass_on(j):
        across[j].wait_recv()
        made = []
        for d in range(1, NY):
            copy = pltpu.make_async_remote_copy(
                src_ref=occ_all.at[partner, pl.ds(j * FB, FB)],
                dst_ref=occ_all.at[partner, pl.ds(j * FB, FB)],
                send_sem=send_fw.at[j, d - 1],
                recv_sem=recv_fw.at[j, d - 1],
                device_id=at_y(d),
                device_id_type=MESH,
            )
            copy.start()
            made.append(copy)
        return made

    for copy in tables:
        copy.wait()
    prepare_plan(tiles_ref, pairs_ref, live_ref, list_ref, owner_ref, plan_made, target_ref)
    plan_copy = pltpu.make_async_copy(plan_made, plan_ref, plan_sem)
    plan_copy.start()
    for copy in own:
        copy.wait_recv()
    own_copy.wait()
    spread(0, range(blocks))
    plan_copy.wait()
    all_groups = acc.shape[0] // GROUP
    multiply(0, range(blocks), 0, all_groups)
    forward = []
    for j in range(blocks + 1):
        if j < blocks:
            forward.append(pass_on(j))
        if j:
            for copy in forward[j - 1]:
                copy.wait_recv()
            spread(1, [j - 1])
    multiply(1, range(blocks), 0, all_groups)
    forward = [copy for made in forward for copy in made]

    per_block = NXC * CAP
    groups = per_block // 8

    def copies_y(i):
        made = []
        for d in range(1, NY):
            for n, (src, dst) in enumerate(((qy, ry), (sy, rsy))):
                made.append(pltpu.make_async_remote_copy(
                    src_ref=src.at[i, d - 1],
                    dst_ref=dst.at[i, d - 1],
                    send_sem=send_y.at[i, n, d - 1],
                    recv_sem=recv_y.at[i, n, d - 1],
                    device_id=at_y(d),
                    device_id_type=MESH,
                ))
        return made

    def copies_a(i, other):
        return [
            pltpu.make_async_remote_copy(
                src_ref=src.at[i, other],
                dst_ref=dst.at[i, zh],
                send_sem=send_a.at[i, n, other],
                recv_sem=recv_a.at[i, n, zh],
                device_id=at_z(i, other),
                device_id_type=MESH,
            )
            for n, (src, dst) in enumerate(((qa, ra), (sa, rsa)))
        ]

    def code(i):
        first = ((zl + offset(i)) % NZL) * per_block
        for d in range(1, NY):
            at = pl.multiple_of(((y + d) % NY) * 16, 16)
            for g in range(groups):
                values = jnp.concatenate(
                    [acc[plan_ref[blocks * fits, first + g * 8 + n], pl.ds(at, 16), :][None] for n in range(8)], axis=0
                )
                whole, scale = coded(values)
                qy[i, d - 1, g * 8 : g * 8 + 8] = whole
                sy[i, d - 1, g] = scale
        for copy in copies_y(i):
            copy.start()

    lower = lax.broadcasted_iota(jnp.int32, (8, OB), 0) < 4
    mine = pl.multiple_of(y * 16, 16)

    def collect(i):
        first = ((zl + offset(i)) % NZL) * per_block
        for copy in copies_y(i):
            copy.wait_recv()
        firsts, seconds = [], []
        for other in range(NXC):
            halves = ([], [])
            for rank in range(CAP):
                n = other * CAP + rank
                tile = acc[plan_ref[blocks * fits, first + n], pl.ds(mine, 16), :]
                for d in range(NY - 1):
                    tile = tile + decoded(ry[i, d, n]) * rsy[i, d, n // 8]
                a, b = tile[:8], tile[8:]
                halves[0].append(jnp.where(lower, a, pltpu.roll(b, 4, 0)))
                halves[1].append(jnp.where(lower, pltpu.roll(a, 4, 0), b))
            firsts.append(jnp.concatenate(halves[0], axis=0)[None])
            seconds.append(jnp.concatenate(halves[1], axis=0)[None])
        for k, values in enumerate((firsts, seconds)):
            whole, scale = coded(jnp.concatenate(values, axis=0))
            qa[i, k] = whole
            sa[i, k] = scale

    def send_on(i):
        for other in range(NZH):
            for copy in copies_a(i, other):
                copy.start()

    def code_one(i, _):
        code(i)
        return 0

    lax.fori_loop(0, NZL, code_one, 0)
    collect(0)
    first_a = copies_a(0, 1 - zh)
    for copy in first_a:
        copy.start()
    ra[0, zh] = qa[0, zh]
    rsa[0, zh] = sa[0, zh]

    def turn(i, _):
        collect(i)
        send_on(i)
        return 0

    lax.fori_loop(1, NZL - 1, turn, 0)
    collect(NZL - 1)
    send_on(NZL - 1)

    def arrived(i, source):
        for n, dst in enumerate((ra, rsa)):
            pltpu.make_async_remote_copy(
                src_ref=dst.at[i, source],
                dst_ref=dst.at[i, source],
                send_sem=send_a.at[i, n, source],
                recv_sem=recv_a.at[i, n, source],
                device_id=at_z(i, source),
                device_id_type=MESH,
            ).wait_recv()

    def later(i, _):
        for source in range(NZH):
            arrived(i, source)
        return 0

    span = NZL // PARTS
    entries = NXC * span * NZH * CAP
    names = lax.broadcasted_iota(jnp.int32, (occs * OWN_CAP, entries), 0)
    copies_b = []

    def send_x(part):
        if part == 0:
            arrived(0, 1 - zh)
        lax.fori_loop(max(part * span, 1), (part + 1) * span, later, 0)
        here = pl.ds(part * span, span)
        made = []
        for d in range(1, NXC):
            other = (xc + d) % NXC
            for n, (src, dst) in enumerate((
                (ra.at[here, :, other], rb.at[part, xc]),
                (rsa.at[here], rsb.at[part, xc]),
            )):
                copy = pltpu.make_async_remote_copy(
                    src_ref=src,
                    dst_ref=dst,
                    send_sem=send_b.at[part, n, d - 1],
                    recv_sem=recv_b.at[part, n, d - 1],
                    device_id=at_x(d),
                    device_id_type=MESH,
                )
                copy.start()
                made.append(copy)
        for i in range(span):
            rb[part, xc, i] = ra[part * span + i, :, xc]
            rsb[part, xc, i] = rsa[part * span + i]
        copies_b.append(made)

    def add_up(part):
        for copy in copies_b[part]:
            copy.wait_recv()

        def expand(source, _):
            for i in range(span):
                for k in range(NZH):
                    value = decoded(rb[part, source, i, k]) * rsb[part, source, i, k]
                    flat[part, pl.ds(pl.multiple_of(((source * span + i) * NZH + k) * 16, 16), 16), :] = value
            return 0

        lax.fori_loop(0, NXC, expand, 0)
        select = (names == target_ref[part : part + 1, :]).astype(jnp.float32)
        for m in range(8):
            total = jnp.dot(
                select, flat[part, pl.ds(m, entries, stride=8), :],
                precision=lax.Precision.HIGHEST, preferred_element_type=jnp.float32,
            )
            if part:
                total += summed[m]
            if part + 1 < PARTS:
                summed[m] = total
                continue
            row = 2 * (m % 4) + m // 4
            for o in range(occs):
                final[o, pl.ds(row, OWN_CAP, stride=8), :] = total[o * OWN_CAP : (o + 1) * OWN_CAP]

    for part in range(PARTS):
        send_x(part)
        if part:
            add_up(part - 1)
    add_up(PARTS - 1)
    copies_b = [copy for made in copies_b for copy in made]
    for o in range(occs):
        out_ref[:, :, o * OB : (o + 1) * OB] = final[o].reshape(OWN_CAP, 8, OB).astype(out_ref.dtype)

    for copy in across + own + forward + copies_b + first_a:
        copy.wait_send()

    def sent_y(i, _):
        for copy in copies_y(i):
            copy.wait_send()
        return 0

    def sent_a(i, _):
        for other in range(NZH):
            for copy in copies_a(i, other):
                copy.wait_send()
        return 0

    lax.fori_loop(0, NZL, sent_y, 0)
    lax.fori_loop(1, NZL, sent_a, 0)


def exchange(row_tiles, row_pairs, live_rows, tile_list, owner_slot, occ, rows):
    i16, f32, bf16 = jnp.int16, jnp.float32, jnp.bfloat16
    blocks, occs = occ.shape[0] // FB, occ.shape[1] // OB
    fits = NY * NZH
    slots = TILES + occs * GROUP
    tables = (row_tiles, row_pairs, live_rows, tile_list, owner_slot.reshape(1, -1))
    dma = pltpu.SemaphoreType.DMA
    vmem = pl.BlockSpec(memory_space=pltpu.VMEM)
    return pl.pallas_call(
        exchange_kernel,
        out_shape=jax.ShapeDtypeStruct((OWN_CAP, AB // fits, occ.shape[1]), bf16),
        in_specs=[pl.BlockSpec(memory_space=pltpu.HBM)] * 7,
        out_specs=vmem,
        scratch_shapes=[
            *[pltpu.VMEM(table.shape, jnp.int32) for table in tables],
            pltpu.VMEM((blocks * fits + 8, 128), jnp.int32),
            pltpu.SMEM((blocks * fits + 8, 128), jnp.int32),
            pltpu.VMEM((PARTS, NXC * NZL // PARTS * NZH * CAP), jnp.int32),
            pltpu.VMEM((fits,) + occ.shape, bf16),
            pltpu.VMEM((occs, fits * blocks * 2 * FB, 2 * OB), bf16),
            pltpu.VMEM(rows.shape, bf16),
            pltpu.VMEM((rows.shape[0] + 1, AB // 2, 2 * FB), bf16),
            pltpu.VMEM((slots, AB, OB), f32),
            pltpu.VMEM((NZL, NY - 1, NXC * CAP, 16, OB), i16),
            pltpu.VMEM((NZL, NY - 1, NXC * CAP // 8, 1, OB), f32),
            pltpu.VMEM((NZL, NY - 1, NXC * CAP, 16, OB), i16),
            pltpu.VMEM((NZL, NY - 1, NXC * CAP // 8, 1, OB), f32),
            pltpu.VMEM((NZL, NZH, NXC, 16, OB), i16),
            pltpu.VMEM((NZL, NZH, 1, OB), f32),
            pltpu.VMEM((NZL, NZH, NXC, 16, OB), i16),
            pltpu.VMEM((NZL, NZH, 1, OB), f32),
            pltpu.VMEM((PARTS, NXC, NZL // PARTS, NZH, 16, OB), i16),
            pltpu.VMEM((PARTS, NXC, NZL // PARTS, NZH, 1, OB), f32),
            pltpu.VMEM((PARTS, NXC * NZL // PARTS * NZH * 16, OB), f32),
            pltpu.VMEM((8, occs * OWN_CAP, OB), f32),
            pltpu.VMEM((occs, OWN_CAP * 8, OB), f32),
            dma((NY - 1,)), dma((NY - 1,)), dma((blocks,)), dma((blocks,)),
            dma((blocks, NY - 1)), dma((blocks, NY - 1)), dma, dma, dma((5,)), dma,
            dma((NZL, 2, NY - 1)), dma((NZL, 2, NY - 1)),
            dma((NZL, 2, NZH)), dma((NZL, 2, NZH)),
            dma((PARTS, 2, NXC - 1)), dma((PARTS, 2, NXC - 1)),
        ],
        compiler_params=pltpu.CompilerParams(collective_id=0, has_side_effects=True, vmem_limit_bytes=58 << 20),
        name="exchange",
    )(*tables, occ, rows)


def prepare_plan(tiles_ref, pairs_ref, live_ref, list_ref, owner_ref, plan_ref, target_ref):
    f32, bf16 = jnp.float32, jnp.bfloat16
    ao = lax.axis_index("ao")
    zl = ao // NXC
    fits, width = tiles_ref.shape
    blocks = pairs_ref.shape[0]
    columns, tiles = list_ref.shape
    aos = owner_ref.shape[1]
    occs = OCCS
    slots = plan_ref.shape[1]
    none = fits * PAIRS

    def at(shape, axis):
        return lax.broadcasted_iota(jnp.int32, shape, axis)

    def dot(a, b):
        return jnp.dot(a.astype(bf16), b.astype(bf16), preferred_element_type=f32)

    def flip(a):
        n = a.shape[1]
        eye = (at((n, n), 0) == at((n, n), 1)).astype(bf16)
        return lax.dot_general(eye, a.astype(bf16), (((1,), (1,)), ((), ())), preferred_element_type=f32)

    def total(mask, value, axis):
        return jnp.sum(jnp.where(mask, value, 0.0), axis=axis, keepdims=True)

    codes = list_ref[pl.ds(ao, 1), :]
    eight = at((8, tiles), 0)
    both = jnp.where(eight == 0, codes & (occs - 1), codes >> OCC_BITS)
    turned = flip(both.astype(f32))
    occ_l = (codes & (occs - 1)).astype(f32)
    occ_s, block_s = turned[:, 0:1], turned[:, 1:2]
    row, lane = at((tiles, tiles), 0), at((tiles, tiles), 1)
    slot_l = total((occ_s == occ_l) & (row < lane), 1.0, 0)
    start = jnp.zeros((1, 1), f32)
    groups = at((1, slots), 1) * GROUP
    group_occ = jnp.zeros((1, slots), f32)
    for o in range(occs):
        slot_l = slot_l + jnp.where(occ_l == o, start, 0.0)
        if o:
            group_occ = group_occ + jnp.where(groups.astype(f32) >= start, 1.0, 0.0)
        count = total(occ_l == o, 1.0, 1)
        start = start + jnp.floor((count + (GROUP - 1)) * (1.0 / GROUP)) * GROUP

    owner_row = owner_ref[...].astype(f32)
    where_s = total(block_s == at((tiles, aos), 1).astype(f32), owner_row, 1)
    owner_s = jnp.floor(where_s * (1.0 / OWN_CAP))
    eye = row == lane
    owner_l = total(eye, owner_s, 0)
    slot_s = total(eye, slot_l, 1)
    place_l = owner_l * CAP + total((owner_s == owner_l) & (row < lane), 1.0, 0)
    place_s = total(eye, place_l, 1)
    wide = at((tiles, slots), 1).astype(f32)
    index = total(place_s == wide, slot_s, 0)

    live_s = total(at((fits, fits), 0) == at((fits, fits), 1), live_ref[...].astype(f32), 1)
    inside = at((fits, width), 1).astype(f32) < live_s
    values = []
    for j in range(blocks):
        pair = pairs_ref[j]
        value = (pair + at((fits, width), 0) * PAIRS - none).astype(f32)
        values.append(jnp.where((pair.astype(f32) >= 0.0) & inside, value, 0.0))
    values = jnp.concatenate(values, axis=0)
    rows_s = flip(tiles_ref[...].astype(f32))
    step_of = at(values.shape, 0) % fits
    by_tile = jnp.zeros((values.shape[0], tiles), f32)
    for s in range(fits):
        hit = (rows_s[:, s : s + 1] == at((width, tiles), 1).astype(f32)).astype(f32)
        by_tile = by_tile + jnp.where(step_of == s, dot(values, hit), 0.0)
    table = dot(by_tile, (slot_s == wide).astype(f32)) + none
    high = values.shape[0]
    plan_ref[0:high, :] = jnp.clip(table.astype(jnp.int32), 0, none)
    last = at((8, slots), 0)
    extra = jnp.where(last == 0, index, jnp.where(last == 1, group_occ, 0.0))
    most = jnp.where(last == 0, TILES + occs * GROUP - 1, occs - 1)
    plan_ref[high : high + 8, :] = jnp.minimum(jnp.maximum(extra.astype(jnp.int32), 0), most)

    mine = (ao * OWN_CAP + at((OWN_CAP, aos), 0)).astype(f32)
    held = total(owner_row == mine, (at((OWN_CAP, aos), 1) + 1).astype(f32), 1) - 1.0
    listed = list_ref[...]
    names = (listed >> OCC_BITS).astype(f32)
    place = jnp.full(names.shape, -1.0, f32)
    for i in range(OWN_CAP):
        place = jnp.where(names == held[i : i + 1, :], float(i), place)
    owned = place >= 0.0
    goal = (listed & (occs - 1)).astype(f32) * OWN_CAP + place
    rank = dot(jnp.where(owned, 1.0, 0.0), (row < lane).astype(f32))
    goals = [total(owned & (rank == r), goal + 1.0, 1) for r in range(CAP)]
    span = NZL // PARTS
    entry = at((columns, target_ref.shape[1]), 1)
    column = at((columns, target_ref.shape[1]), 0)
    rank_of, turn = entry % CAP, entry // (CAP * NZH) % span
    side = entry // (CAP * NZH * span)
    for part in range(PARTS):
        k = part * span + turn
        source = (zl - offset(k) + NZL) % NZL * NXC + side
        goal_of = jnp.where(rank_of == 0, goals[0], goals[1])
        target_ref[part : part + 1, :] = (total(column == source, goal_of, 0) - 1.0).astype(jnp.int32)


def shards(occ_blocks, resident, row_tiles, row_pairs, live_rows, tile_list, owner_slot):
    return exchange(row_tiles[0], row_pairs[:, 0], live_rows, tile_list, owner_slot, occ_blocks, resident)


def solution(mesh):
    return jax.shard_map(
        shards,
        mesh=mesh,
        in_specs=(
            P(("fit", "ao"), None),
            P(("fit", "ao"), None),
            P(("fit", "ao"), None, None),
            P(None, ("fit", "ao"), None, None),
            P(("fit", "ao"), None),
            P(),
            P(),
        ),
        out_specs=P("ao", "fit", None),
        check_vma=False,
    )
```
